32 devices in a mesh: groups: 2 (over x), rows: 16 (over z, y, core).
Axes of the slice: x: 2, y: 2, z: 4, core: 2. Of those that a mesh axis runs over, the one named last changes fastest.
Arguments:
- pixels: bfloat16 [128, 16, 512], P(('groups', 'rows')), parts along dimension 0, may hold values from -6 to 6
- weight_first: bfloat16 [3, 3, 512, 512], replicated, may hold values from -0.09375 to 0.09375
- weight_second: bfloat16 [3, 3, 512, 512], replicated, may hold values from -0.09375 to 0.09375
- weight_mix: bfloat16 [3, 3, 2048, 2048], P(None, None, None, 'rows'), may hold values from -0.046875 to 0.046875
- weight_out: bfloat16 [3, 3, 2048, 2048], P(None, None, 'rows'), may hold values from -0.046875 to 0.046875
Outputs:
- latent_out: bfloat16 [32, 4, 2048], P(('groups', 'rows')), parts along dimension 0
The draws below stay inside these ranges and needn't reach their ends.
There are 2 independent parts, one for each index of `groups`. The reference program is written for one: setup_inputs(seed, part) draws one part's arguments, and reference() takes and returns one part's arrays. A program takes and returns all parts, laid end to end along the dimension named above; an argument that names none is the same for every part. Nothing has to cross between parts.
All inputs are finite; a program needn't handle non-finite values.
Results may differ from the reference program's by a relative error of at most 0.014.
Values may be sent and summed in bfloat16 or wider, within the bound.
No kernel may reach another device: no remote copies, remote signals or barrier semaphores. Data moves between devices by JAX's collectives and lax.ppermute only.
A program may use at most 64 MiB of HBM per device.

```python
import jax
import jax.numpy as jnp

CH = 512
WD = 16
CL = 2048
HT = 64


def block_scale(stream_key, shape, shards, least, top_value):
    level, own = 1.0, jax.random.fold_in(stream_key, 6)
    for dim, parts in shards:
        heights = jnp.exp(jax.random.uniform(jax.random.fold_in(own, dim), (parts,), jnp.float32, least / len(shards), top_value / len(shards)))
        level = level * jnp.repeat(heights, shape[dim] // parts).reshape([-1 if axis == dim else 1 for axis in range(len(shape))])
    return level


def scatter_about(own_key, shape, scale, most, shards=(), kind=jnp.bfloat16):
    entries = scale * jax.random.normal(own_key, shape, jnp.float32)
    if shards:
        entries = entries * block_scale(own_key, shape, shards, -0.22, 0.18)
    return jnp.clip(entries, -most, most).astype(kind)


def setup_inputs(seed: int = 0, part: int = 0) -> dict:
    key_of = jax.random.split(jax.random.key(seed), 6)
    part_keys = jax.random.split(jax.random.fold_in(key_of[5], part), 6)
    pixels = scatter_about(part_keys[0], (HT, WD, CH), 1.0, 6.0, ((0, 16),))
    weight_first = scatter_about(key_of[1], (3, 3, CH, CH), (9 * CH) ** -0.5, 0.09375)
    weight_second = scatter_about(key_of[2], (3, 3, CH, CH), (9 * CH) ** -0.5, 0.09375)
    weight_mix = scatter_about(key_of[3], (3, 3, CL, CL), (9 * CL) ** -0.5, 0.046875, ((3, 16),))
    weight_out = scatter_about(key_of[4], (3, 3, CL, CL), (9 * CL) ** -0.5, 0.046875, ((2, 16),))
    return dict(pixels=pixels, weight_first=weight_first, weight_second=weight_second, weight_mix=weight_mix, weight_out=weight_out)


def conv_same(feature, weight):
    padded = jnp.pad(feature, ((1, 1), (1, 1), (0, 0)))
    row_count = feature.shape[0]
    col_count = feature.shape[1]
    summed = jnp.zeros((row_count, col_count, weight.shape[3]), jnp.float32)
    for row_tap in range(3):
        for col_tap in range(3):
            summed = summed + jnp.dot(padded[row_tap:row_tap + row_count, col_tap:col_tap + col_count], weight[row_tap, col_tap], preferred_element_type=jnp.float32)
    return summed


def unshuffle_average(feature):
    row_count, col_count, chan_count = feature.shape
    widened = feature.astype(jnp.float32).reshape(row_count // 2, 2, col_count // 2, 2, chan_count)
    paired = (widened[:, :, :, 0] + widened[:, :, :, 1]) * 0.5
    return jnp.transpose(paired, (0, 2, 3, 1)).reshape(row_count // 2, col_count // 2, 2 * chan_count).astype(jnp.bfloat16)


def reference(pixels, weight_first, weight_second, weight_mix, weight_out):
    activated = jax.nn.silu(conv_same(pixels, weight_first)).astype(jnp.bfloat16)
    block_out = (pixels.astype(jnp.float32) + conv_same(activated, weight_second)).astype(jnp.bfloat16)
    half_res = unshuffle_average(block_out)
    latent = unshuffle_average(half_res)
    hidden = jax.nn.silu(conv_same(latent, weight_mix)).astype(jnp.bfloat16)
    return (latent.astype(jnp.float32) + conv_same(hidden, weight_out)).astype(jnp.bfloat16)
```

```python
import functools

import jax
import jax.numpy as jnp
from jax import lax
from jax.experimental import pallas as pl
from jax.experimental.pallas import tpu as pltpu
from jax.sharding import PartitionSpec as P

F32 = jnp.float32
BF16 = jnp.bfloat16
LOW = 4
LOW_ORDER = (0, 2, 1, 3)
LANES = 128
VMEM = pl.BlockSpec(memory_space=pltpu.VMEM)
SMEM = pl.BlockSpec(memory_space=pltpu.SMEM)


def silu(value):
    return value / (1.0 + jnp.exp(-value))


def shift_cols(value, step, width):
    if step == 0:
        return value
    count = value.shape[0]
    moved = pltpu.roll(value, (-step) % count, 0)
    col = lax.broadcasted_iota(jnp.int32, value.shape, 0) % width
    keep = (col + step >= 0) & (col + step < width)
    return jnp.where(keep, moved, 0.0)


def conv_image(feature, weight_ref, width):
    out_rows = feature.shape[0] - 2 * width
    total = None
    for col_tap in (1, 0, 2):
        term = None
        for row_tap in range(3):
            part = jnp.dot(
                feature[row_tap * width : row_tap * width + out_rows],
                weight_ref[row_tap, col_tap],
                preferred_element_type=F32,
            )
            term = part if term is None else term + part
        term = shift_cols(term, col_tap - 1, width)
        total = term if total is None else total + term
    return total


def image_kernel(edge_ref, before_ref, pixels_ref, after_ref, first_ref, second_ref, latent_ref, wide_ref, packed_ref):
    rows, width, chans = pixels_ref.shape
    flat = lambda ref: ref[...].reshape(ref.shape[0] * width, chans)
    pixels = flat(pixels_ref)
    extended = jnp.concatenate([flat(before_ref), pixels, flat(after_ref)], axis=0)
    activated = silu(conv_image(extended, first_ref, width)).astype(BF16).astype(F32)
    row = lax.broadcasted_iota(jnp.int32, activated.shape, 0) // width
    inside = (row >= edge_ref[0]) & (row < edge_ref[1])
    activated = jnp.where(inside, activated, 0.0).astype(BF16)
    block = pixels.astype(F32) + conv_image(activated, second_ref, width)
    block = block.astype(BF16).astype(F32)
    count = rows * width
    half = ((block + pltpu.roll(block, count - 1, 0)) * 0.5).astype(BF16).astype(F32)
    quarter = ((half + pltpu.roll(half, count - 2, 0)) * 0.5).astype(BF16).astype(F32)
    chunks = chans // LANES
    cols = width // 4
    for chunk in range(chunks):
        wide_ref[chunk] = quarter[:, chunk * LANES : (chunk + 1) * LANES]
    source = lax.broadcasted_iota(jnp.int32, (4 * LANES, 4 * LANES), 0)
    target = lax.broadcasted_iota(jnp.int32, (4 * LANES, 4 * LANES), 1)
    r = source // LANES
    place = (target == 4 * (source % LANES) + 2 * (r % 2) + r // 2).astype(F32).astype(BF16)
    for out_row in range(rows // 4):
        for chunk in range(chunks):
            for sub in range(4):
                start = (4 * out_row + sub) * width
                packed_ref[chunk * cols : (chunk + 1) * cols, sub * LANES : (sub + 1) * LANES] = wide_ref[
                    chunk, pl.ds(start, cols, stride=4), :
                ]
        spread = jnp.dot(packed_ref[...].astype(BF16), place, preferred_element_type=F32)
        for chunk in range(chunks):
            latent_ref[out_row, :, chunk * 4 * LANES : (chunk + 1) * 4 * LANES] = spread[
                chunk * cols : (chunk + 1) * cols
            ].astype(BF16)


def image_stage(pixels, before, after, edges, weight_first, weight_second):
    rows, width, chans = pixels.shape
    flops = 2 * 9 * width * chans * chans * (2 * rows + 2)
    moved = 2 * (weight_first.size + weight_second.size + 3 * pixels.size)
    return pl.pallas_call(
        image_kernel,
        out_shape=jax.ShapeDtypeStruct((rows // 4, width // 4, 4 * chans), BF16),
        in_specs=[SMEM] + [VMEM] * 5,
        out_specs=VMEM,
        scratch_shapes=[
            pltpu.VMEM((chans // LANES, rows * width, LANES), F32),
            pltpu.VMEM((chans // LANES * (width // 4), 4 * LANES), F32),
        ],
        compiler_params=pltpu.CompilerParams(vmem_limit_bytes=20 << 20),
        cost_estimate=pl.CostEstimate(flops=flops, bytes_accessed=moved, transcendentals=rows * width * chans),
        name="image_stage",
    )(edges, before, pixels, after, weight_first, weight_second)


def shift_rows(value, step, block, cols):
    if step == 0:
        return value
    pieces = [value[LOW_ORDER[u] * block : (LOW_ORDER[u] + 1) * block] for u in range(LOW)]
    high = lax.broadcasted_iota(jnp.int32, pieces[0].shape, 0) // cols
    if step > 0:
        wrapped = jnp.where(high < block // cols - 1, pltpu.roll(pieces[0], block - cols, 0), 0.0)
        pieces = pieces[1:] + [wrapped]
    else:
        wrapped = jnp.where(high > 0, pltpu.roll(pieces[-1], cols, 0), 0.0)
        pieces = [wrapped] + pieces[:-1]
    return jnp.concatenate([pieces[u] for u in LOW_ORDER], axis=0)


def latent_kernel(cols, gathered_ref, mix_ref, out_ref, total_ref):
    low, block, chans = gathered_ref.shape
    feature = gathered_ref[...].reshape(low * block, chans)
    hidden_count = mix_ref.shape[3]
    taps = [(a, b) for a in range(3) for b in range(3)]
    terms = {}
    for start in range(0, 9, 2):
        pair = taps[start : start + 2]
        weight = jnp.concatenate([mix_ref[a, b] for a, b in pair], axis=1)
        both = jnp.dot(feature, weight, preferred_element_type=F32)
        for slot, tap in enumerate(pair):
            terms[tap] = both[:, slot * hidden_count : (slot + 1) * hidden_count]
    summed = None
    for a in range(3):
        line = terms[a, 1] + shift_cols(terms[a, 0], -1, cols) + shift_cols(terms[a, 2], 1, cols)
        line = shift_rows(line, a - 1, block, cols)
        summed = line if summed is None else summed + line
    hidden = silu(summed).astype(BF16).astype(F32)
    moved = []
    for a in range(3):
        line = shift_rows(hidden, a - 1, block, cols)
        for b in range(3):
            moved.append(shift_cols(line, b - 1, cols).astype(BF16))
    stacked = jnp.concatenate(moved, axis=1)
    weight = out_ref[...].reshape(9 * hidden_count, out_ref.shape[3])
    total = jnp.dot(stacked, weight, preferred_element_type=F32)
    total_ref[...] = total.reshape(low, block, chans)


def latent_stage(gathered, weight_mix, weight_out, cols):
    low, block, chans = gathered.shape
    flops = 2 * low * block * (weight_mix.size + weight_out.size)
    moved = 2 * (weight_mix.size + weight_out.size) + 6 * gathered.size
    return pl.pallas_call(
        functools.partial(latent_kernel, cols),
        out_shape=jax.ShapeDtypeStruct((low, block, chans), F32),
        in_specs=[VMEM] * 3,
        out_specs=VMEM,
        compiler_params=pltpu.CompilerParams(vmem_limit_bytes=20 << 20),
        cost_estimate=pl.CostEstimate(flops=flops, bytes_accessed=moved, transcendentals=low * block * weight_mix.shape[3]),
        name="latent_stage",
    )(gathered, weight_mix, weight_out)


def swap(value, peers, bit):
    return lax.ppermute(value, "rows", [(i, i ^ bit) for i in range(peers)])


def ordered(own, got, upper, axis):
    low, high = jnp.where(upper, got, own), jnp.where(upper, own, got)
    return jnp.concatenate([low, high], axis=axis)


def gather_rows(latent, peers, me):
    held = latent[0]
    bit = LOW
    while bit < peers:
        got = swap(held, peers, bit)
        held = ordered(held, got, (me & bit) != 0, 0)
        bit *= 2
    held = held[None]
    bit = LOW // 2
    while bit:
        got = swap(held, peers, bit)
        held = ordered(held, got, (me & bit) != 0, 0)
        bit //= 2
    return held


def halved(held, peers, me, bit):
    half = held.shape[0] // 2
    own = (me // bit) % 2
    keep = lax.dynamic_slice_in_dim(held, own * half, half, 0)
    send = lax.dynamic_slice_in_dim(held, (1 - own) * half, half, 0).astype(BF16)
    return keep + swap(send, peers, bit).astype(F32)


def scatter_sum(total, peers, me, cols):
    held = total
    bit = 1
    while bit < LOW:
        held = halved(held, peers, me, bit)
        bit *= 2
    held = held[0]
    bit = peers // 2
    while bit >= LOW:
        held = halved(held, peers, me, bit)
        bit //= 2
    return held


def plain_latent(latent, weight_mix, weight_out):
    whole = lax.all_gather(latent, "rows", axis=0, tiled=True)

    def conv(value, weight):
        rows, cols = value.shape[:2]
        padded = jnp.pad(value, ((1, 1), (1, 1), (0, 0)))
        summed = 0.0
        for a in range(3):
            for b in range(3):
                summed = summed + jnp.dot(
                    padded[a : a + rows, b : b + cols], weight[a, b], preferred_element_type=F32
                )
        return summed

    hidden = jax.nn.silu(conv(whole, weight_mix)).astype(BF16)
    mixed = lax.psum_scatter(conv(hidden, weight_out), "rows", scatter_dimension=0, tiled=True)
    return (latent.astype(F32) + mixed).astype(BF16)


def local(pixels, weight_first, weight_second, weight_mix, weight_out):
    peers = lax.axis_size("rows")
    me = lax.axis_index("rows")
    rows = pixels.shape[0]
    up = [(i, i + 1) for i in range(peers - 1)]
    before = lax.ppermute(pixels[rows - 2 :], "rows", up)
    after = lax.ppermute(pixels[:2], "rows", [(j, i) for i, j in up])
    edges = jnp.stack([jnp.where(me == 0, 1, 0), jnp.where(me == peers - 1, rows + 1, rows + 2)]).astype(jnp.int32)
    latent = image_stage(pixels, before, after, edges, weight_first, weight_second)
    power = peers >= 2 * LOW and peers & (peers - 1) == 0
    if not power or latent.shape[0] != 1 or weight_mix.shape[3] % LANES:
        return plain_latent(latent, weight_mix, weight_out)
    cols = latent.shape[1]
    gathered = gather_rows(latent, peers, me)
    total = latent_stage(gathered, weight_mix, weight_out, cols)
    mixed = scatter_sum(total, peers, me, cols)
    return (latent.astype(F32) + mixed[None]).astype(BF16)


def solution(mesh):
    return jax.shard_map(
        local,
        mesh=mesh,
        in_specs=(
            P(("groups", "rows"), None, None),
            P(),
            P(),
            P(None, None, None, "rows"),
            P(None, None, "rows", None),
        ),
        out_specs=P(("groups", "rows"), None, None),
        check_vma=False,
    )
```

```python
import functools

import jax
import jax.numpy as jnp
from jax import lax
from jax.experimental import pallas as pl
from jax.experimental.pallas import tpu as pltpu
from jax.sharding import PartitionSpec as P

F32 = jnp.float32
BF16 = jnp.bfloat16
LOW = 4
LOW_ORDER = (0, 2, 1, 3)
LANES = 128
VMEM = pl.BlockSpec(memory_space=pltpu.VMEM)
COVER = 2 * 10**10


def silu(value):
    return value / (1.0 + jnp.exp(-value))


def flag_of(flags_ref, index):
    return flags_ref[index, :1, :1] != 0


def pick(flag, one, other):
    return jnp.where(flag, one.astype(F32), other.astype(F32))


def place_kernel(bits, last, me_ref, pixels_ref, inner_ref, outer_ref, flags_ref):
    me = me_ref[...]
    for bit in range(bits):
        flags_ref[bit] = (me >> bit) & 1
    flags_ref[bits] = (me == 0).astype(jnp.int32)
    flags_ref[bits + 1] = (me == last).astype(jnp.int32)
    odd = (me & 1)[:1, :1] != 0
    rows, edge = pixels_ref.shape[0], inner_ref.shape[0]
    for row in range(edge):
        top, bottom = pixels_ref[row], pixels_ref[rows - edge + row]
        inner_ref[row] = pick(odd, top, bottom).astype(inner_ref.dtype)
        outer_ref[row] = pick(odd, bottom, top).astype(outer_ref.dtype)


def placed(me, peers, pixels, edge):
    bits = max(1, (peers - 1).bit_length())
    rows = jax.ShapeDtypeStruct((edge, *pixels.shape[1:]), pixels.dtype)
    return pl.pallas_call(
        functools.partial(place_kernel, bits, peers - 1),
        out_shape=[rows, rows, jax.ShapeDtypeStruct((bits + 2, 8, LANES), jnp.int32)],
        in_specs=[VMEM] * 2,
        out_specs=[VMEM] * 3,
        compiler_params=pltpu.CompilerParams(vmem_limit_bytes=2 << 20),
        cost_estimate=pl.CostEstimate(flops=COVER, bytes_accessed=0, transcendentals=0),
        name="place",
    )(jnp.broadcast_to(me, (8, LANES)), pixels)


def shift_cols(value, step, width):
    if step == 0:
        return value
    count = value.shape[0]
    moved = pltpu.roll(value, (-step) % count, 0)
    col = lax.broadcasted_iota(jnp.int32, value.shape, 0) % width
    keep = (col + step >= 0) & (col + step < width)
    return jnp.where(keep, moved, 0.0)


def conv_image(feature, weight_ref, width):
    out_rows = feature.shape[0] - 2 * width
    total = None
    for col_tap in (1, 0, 2):
        term = None
        for row_tap in range(3):
            part = jnp.dot(
                feature[row_tap * width : row_tap * width + out_rows],
                weight_ref[row_tap, col_tap],
                preferred_element_type=F32,
            )
            term = part if term is None else term + part
        term = shift_cols(term, col_tap - 1, width)
        total = term if total is None else total + term
    return total


def image_kernel(flags_ref, inner_ref, outer_ref, pixels_ref, first_ref, second_ref, latent_ref, wide_ref, packed_ref):
    rows, width, chans = pixels_ref.shape
    flat = lambda ref: ref[...].reshape(ref.shape[0] * width, chans)
    pixels = flat(pixels_ref)
    odd, bits = flag_of(flags_ref, 0), flags_ref.shape[0] - 2
    inner, outer = flat(inner_ref), flat(outer_ref)
    before, after = pick(odd, inner, outer).astype(BF16), pick(odd, outer, inner).astype(BF16)
    extended = jnp.concatenate([before, pixels, after], axis=0)
    activated = silu(conv_image(extended, first_ref, width)).astype(BF16).astype(F32)
    row = lax.broadcasted_iota(jnp.int32, activated.shape, 0) // width
    inside = (row >= flags_ref[bits, :1, :1]) & (row < rows + 2 - flags_ref[bits + 1, :1, :1])
    activated = jnp.where(inside, activated, 0.0).astype(BF16)
    block = pixels.astype(F32) + conv_image(activated, second_ref, width)
    block = block.astype(BF16).astype(F32)
    count = rows * width
    half = ((block + pltpu.roll(block, count - 1, 0)) * 0.5).astype(BF16).astype(F32)
    quarter = ((half + pltpu.roll(half, count - 2, 0)) * 0.5).astype(BF16).astype(F32)
    chunks = chans // LANES
    cols = width // 4
    for chunk in range(chunks):
        wide_ref[chunk] = quarter[:, chunk * LANES : (chunk + 1) * LANES]
    source = lax.broadcasted_iota(jnp.int32, (4 * LANES, 4 * LANES), 0)
    target = lax.broadcasted_iota(jnp.int32, (4 * LANES, 4 * LANES), 1)
    r = source // LANES
    place = (target == 4 * (source % LANES) + 2 * (r % 2) + r // 2).astype(F32).astype(BF16)
    for out_row in range(rows // 4):
        for chunk in range(chunks):
            for sub in range(4):
                start = (4 * out_row + sub) * width
                packed_ref[chunk * cols : (chunk + 1) * cols, sub * LANES : (sub + 1) * LANES] = wide_ref[
                    chunk, pl.ds(start, cols, stride=4), :
                ]
        spread = jnp.dot(packed_ref[...].astype(BF16), place, preferred_element_type=F32)
        for chunk in range(chunks):
            latent_ref[out_row, :, chunk * 4 * LANES : (chunk + 1) * 4 * LANES] = spread[
                chunk * cols : (chunk + 1) * cols
            ].astype(BF16)


def image_stage(flags, inner, outer, pixels, weight_first, weight_second):
    rows, width, chans = pixels.shape
    flops = 2 * 9 * width * chans * chans * (2 * rows + 2)
    moved = 2 * (weight_first.size + weight_second.size + 3 * pixels.size)
    return pl.pallas_call(
        image_kernel,
        out_shape=jax.ShapeDtypeStruct((rows // 4, width // 4, 4 * chans), BF16),
        in_specs=[VMEM] * 6,
        out_specs=VMEM,
        scratch_shapes=[
            pltpu.VMEM((chans // LANES, rows * width, LANES), F32),
            pltpu.VMEM((chans // LANES * (width // 4), 4 * LANES), F32),
        ],
        compiler_params=pltpu.CompilerParams(vmem_limit_bytes=20 << 20),
        cost_estimate=pl.CostEstimate(flops=flops, bytes_accessed=moved, transcendentals=rows * width * chans),
        name="image_stage",
    )(flags, inner, outer, pixels, weight_first, weight_second)


def shift_rows(value, step, block, cols):
    if step == 0:
        return value
    pieces = [value[LOW_ORDER[u] * block : (LOW_ORDER[u] + 1) * block] for u in range(LOW)]
    high = lax.broadcasted_iota(jnp.int32, pieces[0].shape, 0) // cols
    if step > 0:
        wrapped = jnp.where(high < block // cols - 1, pltpu.roll(pieces[0], block - cols, 0), 0.0)
        pieces = pieces[1:] + [wrapped]
    else:
        wrapped = jnp.where(high > 0, pltpu.roll(pieces[-1], cols, 0), 0.0)
        pieces = [wrapped] + pieces[:-1]
    return jnp.concatenate([pieces[u] for u in LOW_ORDER], axis=0)


def halve(total, upper, inner, keep_ref, send_ref):
    for pair in range(total.shape[0] // (2 * inner)):
        first = total[2 * pair * inner : (2 * pair + 1) * inner]
        second = total[(2 * pair + 1) * inner : (2 * pair + 2) * inner]
        keep_ref[pair * inner : (pair + 1) * inner] = pick(upper, second, first)
        send_ref[pair * inner : (pair + 1) * inner] = pick(upper, first, second).astype(send_ref.dtype)


def latent_kernel(cols, flags_ref, gathered_ref, mix_ref, out_ref, keep_ref, send_ref):
    feature = gathered_ref[...]
    block = feature.shape[0] // LOW
    hidden_count = mix_ref.shape[3]
    taps = [(a, b) for a in range(3) for b in range(3)]
    terms = {}
    for start in range(0, 9, 2):
        pair = taps[start : start + 2]
        weight = jnp.concatenate([mix_ref[a, b] for a, b in pair], axis=1)
        both = jnp.dot(feature, weight, preferred_element_type=F32)
        for slot, tap in enumerate(pair):
            terms[tap] = both[:, slot * hidden_count : (slot + 1) * hidden_count]
    summed = None
    for a in range(3):
        line = terms[a, 1] + shift_cols(terms[a, 0], -1, cols) + shift_cols(terms[a, 2], 1, cols)
        line = shift_rows(line, a - 1, block, cols)
        summed = line if summed is None else summed + line
    hidden = silu(summed).astype(BF16).astype(F32)
    moved = []
    for a in range(3):
        line = shift_rows(hidden, a - 1, block, cols)
        for b in range(3):
            moved.append(shift_cols(line, b - 1, cols).astype(BF16))
    stacked = jnp.concatenate(moved, axis=1)
    weight = out_ref[...].reshape(9 * hidden_count, out_ref.shape[3])
    total = jnp.dot(stacked, weight, preferred_element_type=F32)
    halve(total, flag_of(flags_ref, 0), feature.shape[0] // 2, keep_ref, send_ref)


def latent_stage(flags, gathered, weight_mix, weight_out, cols):
    count, chans = gathered.shape
    flops = 2 * count * (weight_mix.size + weight_out.size)
    moved = 2 * (weight_mix.size + weight_out.size) + 6 * gathered.size
    return pl.pallas_call(
        functools.partial(latent_kernel, cols),
        out_shape=[jax.ShapeDtypeStruct((count // 2, chans), kind) for kind in (F32, BF16)],
        in_specs=[VMEM] * 4,
        out_specs=[VMEM] * 2,
        compiler_params=pltpu.CompilerParams(vmem_limit_bytes=20 << 20),
        cost_estimate=pl.CostEstimate(flops=flops, bytes_accessed=moved, transcendentals=count * weight_mix.shape[3]),
        name="latent_stage",
    )(flags, gathered, weight_mix, weight_out)


def swap(value, peers, bit):
    return lax.ppermute(value, "rows", [(i, i ^ bit) for i in range(peers)])


def halo(inner, outer, peers):
    pairs = [(i, i + 1) for i in range(0, peers - 1, 2)], [(i, i + 1) for i in range(1, peers - 1, 2)]
    both = [one + [(j, i) for i, j in one] for one in pairs]
    return lax.ppermute(inner, "rows", both[0]), lax.ppermute(outer, "rows", both[1])


def merge_kernel(index, inner, flags_ref, own_ref, got_ref, both_ref):
    upper = flag_of(flags_ref, index)
    own, got = own_ref[...].astype(F32), got_ref[...].astype(F32)
    for block in range(own.shape[0] // inner):
        mine, other = own[block * inner : (block + 1) * inner], got[block * inner : (block + 1) * inner]
        start = 2 * block * inner
        both_ref[start : start + inner] = jnp.where(upper, other, mine).astype(both_ref.dtype)
        both_ref[start + inner : start + 2 * inner] = jnp.where(upper, mine, other).astype(both_ref.dtype)


def merged(flags, own, got, index, inner, cover=0):
    return pl.pallas_call(
        functools.partial(merge_kernel, index, inner),
        out_shape=jax.ShapeDtypeStruct((2 * own.shape[0], own.shape[1]), own.dtype),
        in_specs=[VMEM] * 3,
        out_specs=VMEM,
        compiler_params=pltpu.CompilerParams(vmem_limit_bytes=2 << 20),
        cost_estimate=pl.CostEstimate(flops=cover, bytes_accessed=8 * own.size, transcendentals=0),
        name="merge",
    )(flags, own, got)


def gather_rows(latent, flags, peers, cols):
    held = latent
    bit = peers // 2
    while bit:
        got = swap(held, peers, bit)
        inner = cols if bit >= LOW else held.shape[0]
        held = merged(flags, held, got, bit.bit_length() - 1, inner, COVER if bit == peers // 2 else 0)
        bit //= 2
    return held


def halve_kernel(index, inner, flags_ref, held_ref, got_ref, keep_ref, send_ref):
    halve(held_ref[...] + got_ref[...].astype(F32), flag_of(flags_ref, index), inner, keep_ref, send_ref)


def halved(flags, held, got, index, inner):
    shape = (held.shape[0] // 2, held.shape[1])
    return pl.pallas_call(
        functools.partial(halve_kernel, index, inner),
        out_shape=[jax.ShapeDtypeStruct(shape, kind) for kind in (F32, BF16)],
        in_specs=[VMEM] * 3,
        out_specs=[VMEM] * 2,
        compiler_params=pltpu.CompilerParams(vmem_limit_bytes=2 << 20),
        cost_estimate=pl.CostEstimate(flops=held.size, bytes_accessed=6 * held.size, transcendentals=0),
        name="halve",
    )(flags, held, got)


def scatter_sum(keep, send, flags, peers, cols):
    bit = 1
    while 2 * bit < peers:
        got = swap(send, peers, bit)
        bit *= 2
        keep, send = halved(flags, keep, got, bit.bit_length() - 1, cols if bit >= LOW else keep.shape[0] // 2)
    return keep + swap(send, peers, bit).astype(F32)


def plain_latent(latent, weight_mix, weight_out):
    whole = lax.all_gather(latent, "rows", axis=0, tiled=True)

    def conv(value, weight):
        rows, cols = value.shape[:2]
        padded = jnp.pad(value, ((1, 1), (1, 1), (0, 0)))
        summed = 0.0
        for a in range(3):
            for b in range(3):
                summed = summed + jnp.dot(
                    padded[a : a + rows, b : b + cols], weight[a, b], preferred_element_type=F32
                )
        return summed

    hidden = jax.nn.silu(conv(whole, weight_mix)).astype(BF16)
    mixed = lax.psum_scatter(conv(hidden, weight_out), "rows", scatter_dimension=0, tiled=True)
    return (latent.astype(F32) + mixed).astype(BF16)


def local(pixels, weight_first, weight_second, weight_mix, weight_out):
    peers = lax.axis_size("rows")
    me = lax.axis_index("rows")
    inner, outer, flags = placed(me, peers, pixels, 2)
    inner, outer = halo(inner, outer, peers)
    latent = image_stage(flags, inner, outer, pixels, weight_first, weight_second)
    power = peers >= 2 * LOW and peers & (peers - 1) == 0
    if not power or latent.shape[0] != 1 or weight_mix.shape[3] % LANES:
        return plain_latent(latent, weight_mix, weight_out)
    cols = latent.shape[1]
    gathered = gather_rows(latent[0], flags, peers, cols)
    keep, send = latent_stage(flags, gathered, weight_mix, weight_out, cols)
    mixed = scatter_sum(keep, send, flags, peers, cols)
    return (latent.astype(F32) + mixed[None]).astype(BF16)


def solution(mesh):
    return jax.shard_map(
        local,
        mesh=mesh,
        in_specs=(
            P(("groups", "rows"), None, None),
            P(),
            P(),
            P(None, None, None, "rows"),
            P(None, None, "rows", None),
        ),
        out_specs=P(("groups", "rows"), None, None),
        check_vma=False,
    )
```

```python
import functools

import jax
import jax.numpy as jnp
from jax import lax
from jax.experimental import pallas as pl
from jax.experimental.pallas import tpu as pltpu
from jax.sharding import PartitionSpec as P

F32 = jnp.float32
BF16 = jnp.bfloat16
LOW = 4
LOW_ORDER = (0, 2, 1, 3)
LANES = 128
VMEM = pl.BlockSpec(memory_space=pltpu.VMEM)
COVER = 2 * 10**10


def silu(value):
    return value / (1.0 + jnp.exp(-value))


def flag_of(flags_ref, index):
    return flags_ref[index, :1, :1] != 0


def pick(flag, one, other):
    return jnp.where(flag, one.astype(F32), other.astype(F32))


def place_kernel(bits, last, me_ref, pixels_ref, inner_ref, outer_ref, flags_ref):
    me = me_ref[...]
    for bit in range(bits):
        flags_ref[bit] = (me >> bit) & 1
    flags_ref[bits] = (me == 0).astype(jnp.int32)
    flags_ref[bits + 1] = (me == last).astype(jnp.int32)
    odd = (me & 1)[:1, :1] != 0
    rows, edge = pixels_ref.shape[0], inner_ref.shape[0]
    for row in range(edge):
        top, bottom = pixels_ref[row], pixels_ref[rows - edge + row]
        inner_ref[row] = pick(odd, top, bottom).astype(inner_ref.dtype)
        outer_ref[row] = pick(odd, bottom, top).astype(outer_ref.dtype)


def placed(me, peers, pixels, edge):
    bits = max(1, (peers - 1).bit_length())
    rows = jax.ShapeDtypeStruct((edge, *pixels.shape[1:]), pixels.dtype)
    return pl.pallas_call(
        functools.partial(place_kernel, bits, peers - 1),
        out_shape=[rows, rows, jax.ShapeDtypeStruct((bits + 2, 8, LANES), jnp.int32)],
        in_specs=[VMEM] * 2,
        out_specs=[VMEM] * 3,
        compiler_params=pltpu.CompilerParams(vmem_limit_bytes=2 << 20),
        cost_estimate=pl.CostEstimate(flops=COVER, bytes_accessed=0, transcendentals=0),
        name="place",
    )(jnp.broadcast_to(me, (8, LANES)), pixels)


def shift_cols(value, step, width):
    if step == 0:
        return value
    count = value.shape[0]
    moved = pltpu.roll(value, (-step) % count, 0)
    col = lax.broadcasted_iota(jnp.int32, value.shape, 0) % width
    keep = (col + step >= 0) & (col + step < width)
    return jnp.where(keep, moved, 0.0)


def conv_image(feature, weight_ref, width):
    out_rows = feature.shape[0] - 2 * width
    total = None
    for col_tap in (1, 0, 2):
        term = None
        for row_tap in range(3):
            part = jnp.dot(
                feature[row_tap * width : row_tap * width + out_rows],
                weight_ref[row_tap, col_tap],
                preferred_element_type=F32,
            )
            term = part if term is None else term + part
        term = shift_cols(term, col_tap - 1, width)
        total = term if total is None else total + term
    return total


def image_kernel(flags_ref, inner_ref, outer_ref, pixels_ref, first_ref, second_ref, latent_ref, wide_ref, packed_ref):
    rows, width, chans = pixels_ref.shape
    flat = lambda ref: ref[...].reshape(ref.shape[0] * width, chans)
    pixels = flat(pixels_ref)
    odd, bits = flag_of(flags_ref, 0), flags_ref.shape[0] - 2
    inner, outer = flat(inner_ref), flat(outer_ref)
    before, after = pick(odd, inner, outer).astype(BF16), pick(odd, outer, inner).astype(BF16)
    extended = jnp.concatenate([before, pixels, after], axis=0)
    activated = silu(conv_image(extended, first_ref, width)).astype(BF16).astype(F32)
    row = lax.broadcasted_iota(jnp.int32, activated.shape, 0) // width
    inside = (row >= flags_ref[bits, :1, :1]) & (row < rows + 2 - flags_ref[bits + 1, :1, :1])
    activated = jnp.where(inside, activated, 0.0).astype(BF16)
    block = pixels.astype(F32) + conv_image(activated, second_ref, width)
    block = block.astype(BF16).astype(F32)
    count = rows * width
    half = ((block + pltpu.roll(block, count - 1, 0)) * 0.5).astype(BF16).astype(F32)
    quarter = ((half + pltpu.roll(half, count - 2, 0)) * 0.5).astype(BF16).astype(F32)
    chunks = chans // LANES
    cols = width // 4
    for chunk in range(chunks):
        wide_ref[chunk] = quarter[:, chunk * LANES : (chunk + 1) * LANES]
    source = lax.broadcasted_iota(jnp.int32, (4 * LANES, 4 * LANES), 0)
    target = lax.broadcasted_iota(jnp.int32, (4 * LANES, 4 * LANES), 1)
    r = source // LANES
    place = (target == 4 * (source % LANES) + 2 * (r % 2) + r // 2).astype(F32).astype(BF16)
    for out_row in range(rows // 4):
        for chunk in range(chunks):
            for sub in range(4):
                start = (4 * out_row + sub) * width
                packed_ref[chunk * cols : (chunk + 1) * cols, sub * LANES : (sub + 1) * LANES] = wide_ref[
                    chunk, pl.ds(start, cols, stride=4), :
                ]
        spread = jnp.dot(packed_ref[...].astype(BF16), place, preferred_element_type=F32)
        for chunk in range(chunks):
            latent_ref[out_row, :, chunk * 4 * LANES : (chunk + 1) * 4 * LANES] = spread[
                chunk * cols : (chunk + 1) * cols
            ].astype(BF16)


def image_stage(flags, inner, outer, pixels, weight_first, weight_second):
    rows, width, chans = pixels.shape
    flops = 2 * 9 * width * chans * chans * (2 * rows + 2)
    moved = 2 * (weight_first.size + weight_second.size + 3 * pixels.size)
    return pl.pallas_call(
        image_kernel,
        out_shape=jax.ShapeDtypeStruct((rows // 4, width // 4, 4 * chans), BF16),
        in_specs=[VMEM] * 6,
        out_specs=VMEM,
        scratch_shapes=[
            pltpu.VMEM((chans // LANES, rows * width, LANES), F32),
            pltpu.VMEM((chans // LANES * (width // 4), 4 * LANES), F32),
        ],
        compiler_params=pltpu.CompilerParams(vmem_limit_bytes=20 << 20),
        cost_estimate=pl.CostEstimate(flops=flops, bytes_accessed=moved, transcendentals=rows * width * chans),
        name="image_stage",
    )(flags, inner, outer, pixels, weight_first, weight_second)


def shift_rows(value, step, block, cols):
    if step == 0:
        return value
    pieces = [value[LOW_ORDER[u] * block : (LOW_ORDER[u] + 1) * block] for u in range(LOW)]
    high = lax.broadcasted_iota(jnp.int32, pieces[0].shape, 0) // cols
    if step > 0:
        wrapped = jnp.where(high < block // cols - 1, pltpu.roll(pieces[0], block - cols, 0), 0.0)
        pieces = pieces[1:] + [wrapped]
    else:
        wrapped = jnp.where(high > 0, pltpu.roll(pieces[-1], cols, 0), 0.0)
        pieces = [wrapped] + pieces[:-1]
    return jnp.concatenate([pieces[u] for u in LOW_ORDER], axis=0)


def halve(total, flags, inner, keep_ref, *send_refs):
    width = len(send_refs) + 1
    for run in range(total.shape[0] // (width * inner)):
        parts = [total[(width * run + k) * inner : (width * run + k + 1) * inner] for k in range(width)]
        for bit, flag in enumerate(flags):
            parts = [jnp.where(flag, parts[k ^ (1 << bit)], parts[k]) for k in range(width)]
        keep_ref[run * inner : (run + 1) * inner] = parts[0]
        for part, send_ref in zip(parts[1:], send_refs):
            send_ref[run * inner : (run + 1) * inner] = part.astype(send_ref.dtype)


def latent_kernel(cols, flags_ref, gathered_ref, mix_ref, out_ref, keep_ref, send_ref):
    feature = gathered_ref[...]
    block = feature.shape[0] // LOW
    hidden_count = mix_ref.shape[3]
    taps = [(a, b) for a in range(3) for b in range(3)]
    terms = {}
    for start in range(0, 9, 2):
        pair = taps[start : start + 2]
        weight = jnp.concatenate([mix_ref[a, b] for a, b in pair], axis=1)
        both = jnp.dot(feature, weight, preferred_element_type=F32)
        for slot, tap in enumerate(pair):
            terms[tap] = both[:, slot * hidden_count : (slot + 1) * hidden_count]
    summed = None
    for a in range(3):
        line = terms[a, 1] + shift_cols(terms[a, 0], -1, cols) + shift_cols(terms[a, 2], 1, cols)
        line = shift_rows(line, a - 1, block, cols)
        summed = line if summed is None else summed + line
    hidden = silu(summed).astype(BF16).astype(F32)
    moved = []
    for a in range(3):
        line = shift_rows(hidden, a - 1, block, cols)
        for b in range(3):
            moved.append(shift_cols(line, b - 1, cols).astype(BF16))
    stacked = jnp.concatenate(moved, axis=1)
    weight = out_ref[...].reshape(9 * hidden_count, out_ref.shape[3])
    total = jnp.dot(stacked, weight, preferred_element_type=F32)
    halve(total, [flag_of(flags_ref, 0)], feature.shape[0] // 2, keep_ref, send_ref)


def latent_stage(flags, gathered, weight_mix, weight_out, cols):
    count, chans = gathered.shape
    flops = 2 * count * (weight_mix.size + weight_out.size)
    moved = 2 * (weight_mix.size + weight_out.size) + 6 * gathered.size
    return pl.pallas_call(
        functools.partial(latent_kernel, cols),
        out_shape=[jax.ShapeDtypeStruct((count // 2, chans), kind) for kind in (F32, BF16)],
        in_specs=[VMEM] * 4,
        out_specs=[VMEM] * 2,
        compiler_params=pltpu.CompilerParams(vmem_limit_bytes=20 << 20),
        cost_estimate=pl.CostEstimate(flops=flops, bytes_accessed=moved, transcendentals=count * weight_mix.shape[3]),
        name="latent_stage",
    )(flags, gathered, weight_mix, weight_out)


def swap(value, peers, bit):
    return lax.ppermute(value, "rows", [(i, i ^ bit) for i in range(peers)])


def halo(inner, outer, peers):
    pairs = [(i, i + 1) for i in range(0, peers - 1, 2)], [(i, i + 1) for i in range(1, peers - 1, 2)]
    both = [one + [(j, i) for i, j in one] for one in pairs]
    return lax.ppermute(inner, "rows", both[0]), lax.ppermute(outer, "rows", both[1])


def merge_kernel(index, inner, flags_ref, *refs):
    *blocks, both_ref = refs
    width = len(blocks)
    flags = [flag_of(flags_ref, index + bit) for bit in range((width - 1).bit_length())]
    values = [ref[...].astype(F32) for ref in blocks]
    for block in range(values[0].shape[0] // inner):
        parts = [value[block * inner : (block + 1) * inner] for value in values]
        for bit, flag in enumerate(flags):
            parts = [jnp.where(flag, parts[k ^ (1 << bit)], parts[k]) for k in range(width)]
        for k, part in enumerate(parts):
            start = (width * block + k) * inner
            both_ref[start : start + inner] = part.astype(both_ref.dtype)


def merged(flags, blocks, index, inner, cover=0):
    rows, chans = blocks[0].shape
    return pl.pallas_call(
        functools.partial(merge_kernel, index, inner),
        out_shape=jax.ShapeDtypeStruct((len(blocks) * rows, chans), blocks[0].dtype),
        in_specs=[VMEM] * (1 + len(blocks)),
        out_specs=VMEM,
        compiler_params=pltpu.CompilerParams(vmem_limit_bytes=2 << 20),
        cost_estimate=pl.CostEstimate(flops=cover, bytes_accessed=8 * blocks[0].size, transcendentals=0),
        name="merge",
    )(flags, *blocks)


def exchanged(values, peers, bit):
    got = {}
    for k in reversed(range(len(values))):
        got[k] = swap(values[k], peers, (k + 1) * bit)
    return [got[k] for k in range(len(values))]


def gather_rows(latent, flags, peers, cols):
    held = latent
    bit = peers // 2
    while bit >= 4 * LOW:
        held = merged(flags, [held, swap(held, peers, bit)], bit.bit_length() - 1, cols)
        bit //= 2
    far = bit // LOW * 2 - 1
    held = merged(flags, [held, *exchanged([held] * far, peers, LOW)], LOW.bit_length() - 1, cols, COVER)
    bit = LOW // 2
    while bit:
        held = merged(flags, [held, swap(held, peers, bit)], bit.bit_length() - 1, held.shape[0])
        bit //= 2
    return held


def halve_kernel(index, inner, flags_ref, held_ref, got_ref, keep_ref, *send_refs):
    flags = [flag_of(flags_ref, index + bit) for bit in range(len(send_refs).bit_length())]
    halve(held_ref[...] + got_ref[...].astype(F32), flags, inner, keep_ref, *send_refs)


def halved(flags, held, got, index, inner, width=2):
    shape = (held.shape[0] // width, held.shape[1])
    keep, *sends = pl.pallas_call(
        functools.partial(halve_kernel, index, inner),
        out_shape=[jax.ShapeDtypeStruct(shape, kind) for kind in [F32] + [BF16] * (width - 1)],
        in_specs=[VMEM] * 3,
        out_specs=[VMEM] * width,
        compiler_params=pltpu.CompilerParams(vmem_limit_bytes=2 << 20),
        cost_estimate=pl.CostEstimate(flops=held.size, bytes_accessed=6 * held.size, transcendentals=0),
        name="halve",
    )(flags, held, got)
    return keep, sends


def scatter_sum(keep, send, flags, peers, cols):
    bit, sends = 1, [send]
    while 2 * bit < LOW:
        got = swap(sends[0], peers, bit)
        bit *= 2
        keep, sends = halved(flags, keep, got, bit.bit_length() - 1, keep.shape[0] // 2)
    got = swap(sends[0], peers, bit)
    high = peers // LOW
    while high > 4:
        high //= 2
        keep, sends = halved(flags, keep, got, (LOW * high).bit_length() - 1, high * cols)
        got = swap(sends[0], peers, LOW * high)
    keep, sends = halved(flags, keep, got, LOW.bit_length() - 1, cols, high)
    for got in exchanged(sends, peers, LOW):
        keep = keep + got.astype(F32)
    return keep


def plain_latent(latent, weight_mix, weight_out):
    whole = lax.all_gather(latent, "rows", axis=0, tiled=True)

    def conv(value, weight):
        rows, cols = value.shape[:2]
        padded = jnp.pad(value, ((1, 1), (1, 1), (0, 0)))
        summed = 0.0
        for a in range(3):
            for b in range(3):
                summed = summed + jnp.dot(
                    padded[a : a + rows, b : b + cols], weight[a, b], preferred_element_type=F32
                )
        return summed

    hidden = jax.nn.silu(conv(whole, weight_mix)).astype(BF16)
    mixed = lax.psum_scatter(conv(hidden, weight_out), "rows", scatter_dimension=0, tiled=True)
    return (latent.astype(F32) + mixed).astype(BF16)


def local(pixels, weight_first, weight_second, weight_mix, weight_out):
    peers = lax.axis_size("rows")
    me = lax.axis_index("rows")
    inner, outer, flags = placed(me, peers, pixels, 2)
    inner, outer = halo(inner, outer, peers)
    latent = image_stage(flags, inner, outer, pixels, weight_first, weight_second)
    power = peers >= 2 * LOW and peers & (peers - 1) == 0
    if not power or latent.shape[0] != 1 or weight_mix.shape[3] % LANES:
        return plain_latent(latent, weight_mix, weight_out)
    cols = latent.shape[1]
    gathered = gather_rows(latent[0], flags, peers, cols)
    keep, send = latent_stage(flags, gathered, weight_mix, weight_out, cols)
    mixed = scatter_sum(keep, send, flags, peers, cols)
    return (latent.astype(F32) + mixed[None]).astype(BF16)


def solution(mesh):
    return jax.shard_map(
        local,
        mesh=mesh,
        in_specs=(
            P(("groups", "rows"), None, None),
            P(),
            P(),
            P(None, None, None, "rows"),
            P(None, None, "rows", None),
        ),
        out_specs=P(("groups", "rows"), None, None),
        check_vma=False,
    )
```

```python
import functools

import jax
import jax.numpy as jnp
from jax import lax
from jax.experimental import pallas as pl
from jax.experimental.pallas import tpu as pltpu
from jax.sharding import PartitionSpec as P


F32 = jnp.float32
BF16 = jnp.bfloat16
LOW = 4
LOW_ORDER = (0, 2, 1, 3)
LANES = 128
VMEM = pl.BlockSpec(memory_space=pltpu.VMEM)
COVER = 2 * 10**10


def silu(value):
    return value / (1.0 + jnp.exp(-value))


def flag_of(flags_ref, index):
    return flags_ref[index, :1, :1] != 0


def pick(flag, one, other):
    return jnp.where(flag, one.astype(F32), other.astype(F32))


def place_kernel(bits, last, me_ref, flags_ref):
    me = me_ref[...]
    for bit in range(bits):
        flags_ref[bit] = (me >> bit) & 1
    flags_ref[bits] = (me == 0).astype(jnp.int32)
    flags_ref[bits + 1] = (me == last).astype(jnp.int32)


def placed(me, peers):
    bits = max(1, (peers - 1).bit_length())
    return pl.pallas_call(
        functools.partial(place_kernel, bits, peers - 1),
        out_shape=jax.ShapeDtypeStruct((bits + 2, 8, LANES), jnp.int32),
        in_specs=[VMEM],
        out_specs=VMEM,
        compiler_params=pltpu.CompilerParams(vmem_limit_bytes=2 << 20),
        cost_estimate=pl.CostEstimate(flops=COVER, bytes_accessed=0, transcendentals=0),
        name="place",
    )(jnp.broadcast_to(me, (8, LANES)))


def shift_cols(value, step, width):
    if step == 0:
        return value
    count = value.shape[0]
    moved = pltpu.roll(value, (-step) % count, 0)
    col = lax.broadcasted_iota(jnp.int32, value.shape, 0) % width
    keep = (col + step >= 0) & (col + step < width)
    return jnp.where(keep, moved, 0.0)


def conv_image(feature, weight_ref, width):
    out_rows = feature.shape[0] - 2 * width
    total = None
    for col_tap in (1, 0, 2):
        term = None
        for row_tap in range(3):
            part = jnp.dot(
                feature[row_tap * width : row_tap * width + out_rows],
                weight_ref[row_tap, col_tap],
                preferred_element_type=F32,
            )
            term = part if term is None else term + part
        term = shift_cols(term, col_tap - 1, width)
        total = term if total is None else total + term
    return total


def image_kernel(flags_ref, inner_ref, outer_ref, pixels_ref, first_ref, second_ref, latent_ref, wide_ref, packed_ref):
    rows, width, chans = pixels_ref.shape
    flat = lambda ref: ref[...].reshape(ref.shape[0] * width, chans)
    pixels = flat(pixels_ref)
    odd, bits = flag_of(flags_ref, 0), flags_ref.shape[0] - 2
    inner, outer = flat(inner_ref), flat(outer_ref)
    edge = 2 * width
    before = pick(odd, inner[-edge:], outer[-edge:]).astype(BF16)
    after = pick(odd, outer[:edge], inner[:edge]).astype(BF16)
    extended = jnp.concatenate([before, pixels, after], axis=0)
    activated = silu(conv_image(extended, first_ref, width)).astype(BF16).astype(F32)
    row = lax.broadcasted_iota(jnp.int32, activated.shape, 0) // width
    inside = (row >= flags_ref[bits, :1, :1]) & (row < rows + 2 - flags_ref[bits + 1, :1, :1])
    activated = jnp.where(inside, activated, 0.0).astype(BF16)
    block = pixels.astype(F32) + conv_image(activated, second_ref, width)
    block = block.astype(BF16).astype(F32)
    count = rows * width
    half = ((block + pltpu.roll(block, count - 1, 0)) * 0.5).astype(BF16).astype(F32)
    quarter = ((half + pltpu.roll(half, count - 2, 0)) * 0.5).astype(BF16).astype(F32)
    chunks = chans // LANES
    cols = width // 4
    for chunk in range(chunks):
        wide_ref[chunk] = quarter[:, chunk * LANES : (chunk + 1) * LANES]
    source = lax.broadcasted_iota(jnp.int32, (4 * LANES, 4 * LANES), 0)
    target = lax.broadcasted_iota(jnp.int32, (4 * LANES, 4 * LANES), 1)
    r = source // LANES
    place = (target == 4 * (source % LANES) + 2 * (r % 2) + r // 2).astype(F32).astype(BF16)
    for out_row in range(rows // 4):
        for chunk in range(chunks):
            for sub in range(4):
                start = (4 * out_row + sub) * width
                packed_ref[chunk * cols : (chunk + 1) * cols, sub * LANES : (sub + 1) * LANES] = wide_ref[
                    chunk, pl.ds(start, cols, stride=4), :
                ]
        spread = jnp.dot(packed_ref[...].astype(BF16), place, preferred_element_type=F32)
        for chunk in range(chunks):
            latent_ref[out_row, :, chunk * 4 * LANES : (chunk + 1) * 4 * LANES] = spread[
                chunk * cols : (chunk + 1) * cols
            ].astype(BF16)


def image_stage(flags, inner, outer, pixels, weight_first, weight_second):
    rows, width, chans = pixels.shape
    flops = 2 * 9 * width * chans * chans * (2 * rows + 2)
    moved = 2 * (weight_first.size + weight_second.size + 3 * pixels.size)
    return pl.pallas_call(
        image_kernel,
        out_shape=jax.ShapeDtypeStruct((rows // 4, width // 4, 4 * chans), BF16),
        in_specs=[VMEM] * 6,
        out_specs=VMEM,
        scratch_shapes=[
            pltpu.VMEM((chans // LANES, rows * width, LANES), F32),
            pltpu.VMEM((chans // LANES * (width // 4), 4 * LANES), F32),
        ],
        compiler_params=pltpu.CompilerParams(vmem_limit_bytes=20 << 20),
        cost_estimate=pl.CostEstimate(flops=flops, bytes_accessed=moved, transcendentals=rows * width * chans),
        name="image_stage",
    )(flags, inner, outer, pixels, weight_first, weight_second)


def shift_rows(value, step, block, cols):
    if step == 0:
        return value
    pieces = [value[LOW_ORDER[u] * block : (LOW_ORDER[u] + 1) * block] for u in range(LOW)]
    high = lax.broadcasted_iota(jnp.int32, pieces[0].shape, 0) // cols
    if step > 0:
        wrapped = jnp.where(high < block // cols - 1, pltpu.roll(pieces[0], block - cols, 0), 0.0)
        pieces = pieces[1:] + [wrapped]
    else:
        wrapped = jnp.where(high > 0, pltpu.roll(pieces[-1], cols, 0), 0.0)
        pieces = [wrapped] + pieces[:-1]
    return jnp.concatenate([pieces[u] for u in LOW_ORDER], axis=0)


def halve(total, flags, inner, keep_ref, *send_refs):
    width = len(send_refs) + 1
    for run in range(total.shape[0] // (width * inner)):
        parts = [total[(width * run + k) * inner : (width * run + k + 1) * inner] for k in range(width)]
        for bit, flag in enumerate(flags):
            parts = [jnp.where(flag, parts[k ^ (1 << bit)], parts[k]) for k in range(width)]
        keep_ref[run * inner : (run + 1) * inner] = parts[0]
        for part, send_ref in zip(parts[1:], send_refs):
            send_ref[run * inner : (run + 1) * inner] = part.astype(send_ref.dtype)


def latent_kernel(cols, flags_ref, gathered_ref, mix_ref, out_ref, keep_ref, send_ref):
    feature = gathered_ref[...]
    block = feature.shape[0] // LOW
    hidden_count = mix_ref.shape[3]
    taps = [(a, b) for a in range(3) for b in range(3)]
    terms = {}
    for start in range(0, 9, 2):
        pair = taps[start : start + 2]
        weight = jnp.concatenate([mix_ref[a, b] for a, b in pair], axis=1)
        both = jnp.dot(feature, weight, preferred_element_type=F32)
        for slot, tap in enumerate(pair):
            terms[tap] = both[:, slot * hidden_count : (slot + 1) * hidden_count]
    summed = None
    for a in range(3):
        line = terms[a, 1] + shift_cols(terms[a, 0], -1, cols) + shift_cols(terms[a, 2], 1, cols)
        line = shift_rows(line, a - 1, block, cols)
        summed = line if summed is None else summed + line
    hidden = silu(summed).astype(BF16).astype(F32)
    moved = []
    for a in range(3):
        line = shift_rows(hidden, a - 1, block, cols)
        for b in range(3):
            moved.append(shift_cols(line, b - 1, cols).astype(BF16))
    stacked = jnp.concatenate(moved, axis=1)
    weight = out_ref[...].reshape(9 * hidden_count, out_ref.shape[3])
    total = jnp.dot(stacked, weight, preferred_element_type=F32)
    halve(total, [flag_of(flags_ref, 0)], feature.shape[0] // 2, keep_ref, send_ref)


def latent_stage(flags, gathered, weight_mix, weight_out, cols):
    count, chans = gathered.shape
    flops = 2 * count * (weight_mix.size + weight_out.size)
    moved = 2 * (weight_mix.size + weight_out.size) + 6 * gathered.size
    return pl.pallas_call(
        functools.partial(latent_kernel, cols),
        out_shape=[jax.ShapeDtypeStruct((count // 2, chans), kind) for kind in (F32, BF16)],
        in_specs=[VMEM] * 4,
        out_specs=[VMEM] * 2,
        compiler_params=pltpu.CompilerParams(vmem_limit_bytes=20 << 20),
        cost_estimate=pl.CostEstimate(flops=flops, bytes_accessed=moved, transcendentals=count * weight_mix.shape[3]),
        name="latent_stage",
    )(flags, gathered, weight_mix, weight_out)


def swap(value, peers, bit):
    return lax.ppermute(value, "rows", [(i, i ^ bit) for i in range(peers)])


def halo(value, peers):
    pairs = [(i, i + 1) for i in range(0, peers - 1, 2)], [(i, i + 1) for i in range(1, peers - 1, 2)]
    both = [one + [(j, i) for i, j in one] for one in pairs]
    outer = lax.ppermute(value, "rows", both[1])
    inner = lax.ppermute(value, "rows", both[0])
    return inner, outer


def merge_kernel(index, inner, flags_ref, *refs):
    *blocks, both_ref = refs
    width = len(blocks)
    flags = [flag_of(flags_ref, index + bit) for bit in range((width - 1).bit_length())]
    values = [ref[...].astype(F32) for ref in blocks]
    for block in range(values[0].shape[0] // inner):
        parts = [value[block * inner : (block + 1) * inner] for value in values]
        for bit, flag in enumerate(flags):
            parts = [jnp.where(flag, parts[k ^ (1 << bit)], parts[k]) for k in range(width)]
        for k, part in enumerate(parts):
            start = (width * block + k) * inner
            both_ref[start : start + inner] = part.astype(both_ref.dtype)


def merged(flags, blocks, index, inner, cover=0):
    rows, chans = blocks[0].shape
    return pl.pallas_call(
        functools.partial(merge_kernel, index, inner),
        out_shape=jax.ShapeDtypeStruct((len(blocks) * rows, chans), blocks[0].dtype),
        in_specs=[VMEM] * (1 + len(blocks)),
        out_specs=VMEM,
        compiler_params=pltpu.CompilerParams(vmem_limit_bytes=2 << 20),
        cost_estimate=pl.CostEstimate(flops=cover, bytes_accessed=8 * blocks[0].size, transcendentals=0),
        name="merge",
    )(flags, *blocks)


def exchanged(values, peers, bit):
    got = []
    for k, value in enumerate(values, 1):
        got.append(swap(value, peers, k * bit))
    return got


def gather_rows(latent, flags, peers, cols):
    held = latent
    bit = peers // 2
    while bit >= 4 * LOW:
        held = merged(flags, [held, swap(held, peers, bit)], bit.bit_length() - 1, cols)
        bit //= 2
    far = bit // LOW * 2 - 1
    held = merged(flags, [held, *exchanged([held] * far, peers, LOW)], LOW.bit_length() - 1, cols, COVER)
    bit = LOW // 2
    while bit:
        held = merged(flags, [held, swap(held, peers, bit)], bit.bit_length() - 1, held.shape[0])
        bit //= 2
    return held


def halve_kernel(index, inner, flags_ref, held_ref, got_ref, keep_ref, *send_refs):
    flags = [flag_of(flags_ref, index + bit) for bit in range(len(send_refs).bit_length())]
    halve(held_ref[...] + got_ref[...].astype(F32), flags, inner, keep_ref, *send_refs)


def halved(flags, held, got, index, inner, width=2):
    shape = (held.shape[0] // width, held.shape[1])
    keep, *sends = pl.pallas_call(
        functools.partial(halve_kernel, index, inner),
        out_shape=[jax.ShapeDtypeStruct(shape, kind) for kind in [F32] + [BF16] * (width - 1)],
        in_specs=[VMEM] * 3,
        out_specs=[VMEM] * width,
        compiler_params=pltpu.CompilerParams(vmem_limit_bytes=2 << 20),
        cost_estimate=pl.CostEstimate(flops=held.size, bytes_accessed=6 * held.size, transcendentals=0),
        name="halve",
    )(flags, held, got)
    return keep, sends


def scatter_sum(keep, send, flags, peers, cols):
    bit, sends = 1, [send]
    while 2 * bit < LOW:
        got = swap(sends[0], peers, bit)
        bit *= 2
        keep, sends = halved(flags, keep, got, bit.bit_length() - 1, keep.shape[0] // 2)
    got = swap(sends[0], peers, bit)
    high = peers // LOW
    while high > 4:
        high //= 2
        keep, sends = halved(flags, keep, got, (LOW * high).bit_length() - 1, high * cols)
        got = swap(sends[0], peers, LOW * high)
    keep, sends = halved(flags, keep, got, LOW.bit_length() - 1, cols, high)
    for got in exchanged(sends, peers, LOW):
        keep = keep + got.astype(F32)
    return keep


def plain_latent(latent, weight_mix, weight_out):
    whole = lax.all_gather(latent, "rows", axis=0, tiled=True)

    def conv(value, weight):
        rows, cols = value.shape[:2]
        padded = jnp.pad(value, ((1, 1), (1, 1), (0, 0)))
        summed = 0.0
        for a in range(3):
            for b in range(3):
                summed = summed + jnp.dot(
                    padded[a : a + rows, b : b + cols], weight[a, b], preferred_element_type=F32
                )
        return summed

    hidden = jax.nn.silu(conv(whole, weight_mix)).astype(BF16)
    mixed = lax.psum_scatter(conv(hidden, weight_out), "rows", scatter_dimension=0, tiled=True)
    return (latent.astype(F32) + mixed).astype(BF16)


def compute(pixels, weight_first, weight_second, weight_mix, weight_out):
    peers = lax.axis_size("rows")
    me = lax.axis_index("rows")
    flags = placed(me, peers)
    inner, outer = halo(pixels, peers)
    latent = image_stage(flags, inner, outer, pixels, weight_first, weight_second)
    power = peers >= 2 * LOW and peers & (peers - 1) == 0
    if not power or latent.shape[0] != 1 or weight_mix.shape[3] % LANES:
        return plain_latent(latent, weight_mix, weight_out)
    cols = latent.shape[1]
    gathered = gather_rows(latent[0], flags, peers, cols)
    keep, send = latent_stage(flags, gathered, weight_mix, weight_out, cols)
    mixed = scatter_sum(keep, send, flags, peers, cols)
    return (latent.astype(F32) + mixed[None]).astype(BF16)


def solution(mesh):
    return jax.shard_map(
        compute,
        mesh=mesh,
        in_specs=(
            P(("groups", "rows"), None, None),
            P(),
            P(),
            P(None, None, None, "rows"),
            P(None, None, "rows", None),
        ),
        out_specs=P(("groups", "rows"), None, None),
        check_vma=False,
    )
```

```python
import functools

import jax
import jax.numpy as jnp
from jax import lax
from jax.experimental import pallas as pl
from jax.experimental.pallas import tpu as pltpu
from jax.sharding import PartitionSpec as P


F32 = jnp.float32
BF16 = jnp.bfloat16
LOW = 4
LOW_ORDER = (0, 2, 1, 3)
LINE = 4
NEAR_FLIP, FAR_FLIP, SIDE_FLIP = 0, 1, 1
LANES = 128
VMEM = pl.BlockSpec(memory_space=pltpu.VMEM)
COVER = 2 * 10**10


def silu(value):
    return value / (1.0 + jnp.exp(-value))


def flag_of(flags_ref, index):
    return flags_ref[index, :1, :1] != 0


def pick(flag, one, other):
    return jnp.where(flag, one.astype(F32), other.astype(F32))


def kind_of(core, side, place):
    return core ^ (SIDE_FLIP * side) ^ (NEAR_FLIP * (place & 1)) ^ (FAR_FLIP * (place >> 1))


def place_kernel(bits, last, me_ref, flags_ref):
    me = me_ref[...]
    for bit in range(bits):
        flags_ref[bit] = (me >> bit) & 1
    flags_ref[bits] = (me == 0).astype(jnp.int32)
    flags_ref[bits + 1] = (me == last).astype(jnp.int32)
    flags_ref[bits + 2] = kind_of(me & 1, (me >> 1) & 1, (me >> 2) & 3)


def placed(me, peers):
    bits = max(1, (peers - 1).bit_length())
    return pl.pallas_call(
        functools.partial(place_kernel, bits, peers - 1),
        out_shape=jax.ShapeDtypeStruct((bits + 3, 8, LANES), jnp.int32),
        in_specs=[VMEM],
        out_specs=VMEM,
        compiler_params=pltpu.CompilerParams(vmem_limit_bytes=2 << 20),
        cost_estimate=pl.CostEstimate(flops=COVER, bytes_accessed=0, transcendentals=0),
        name="place",
    )(jnp.broadcast_to(me, (8, LANES)))


def shift_cols(value, step, width):
    if step == 0:
        return value
    count = value.shape[0]
    moved = pltpu.roll(value, (-step) % count, 0)
    col = lax.broadcasted_iota(jnp.int32, value.shape, 0) % width
    keep = (col + step >= 0) & (col + step < width)
    return jnp.where(keep, moved, 0.0)


def conv_image(feature, weight_ref, width):
    out_rows = feature.shape[0] - 2 * width
    total = None
    for col_tap in (1, 0, 2):
        term = None
        for row_tap in range(3):
            part = jnp.dot(
                feature[row_tap * width : row_tap * width + out_rows],
                weight_ref[row_tap, col_tap],
                preferred_element_type=F32,
            )
            term = part if term is None else term + part
        term = shift_cols(term, col_tap - 1, width)
        total = term if total is None else total + term
    return total


def image_kernel(flags_ref, inner_ref, outer_ref, pixels_ref, first_ref, second_ref, latent_ref, wide_ref, packed_ref):
    rows, width, chans = pixels_ref.shape
    flat = lambda ref: ref[...].reshape(ref.shape[0] * width, chans)
    pixels = flat(pixels_ref)
    odd, bits = flag_of(flags_ref, 0), flags_ref.shape[0] - 3
    inner, outer = flat(inner_ref), flat(outer_ref)
    edge = 2 * width
    before = pick(odd, inner[-edge:], outer[-edge:]).astype(BF16)
    after = pick(odd, outer[:edge], inner[:edge]).astype(BF16)
    extended = jnp.concatenate([before, pixels, after], axis=0)
    activated = silu(conv_image(extended, first_ref, width)).astype(BF16).astype(F32)
    row = lax.broadcasted_iota(jnp.int32, activated.shape, 0) // width
    inside = (row >= flags_ref[bits, :1, :1]) & (row < rows + 2 - flags_ref[bits + 1, :1, :1])
    activated = jnp.where(inside, activated, 0.0).astype(BF16)
    block = pixels.astype(F32) + conv_image(activated, second_ref, width)
    block = block.astype(BF16).astype(F32)
    count = rows * width
    half = ((block + pltpu.roll(block, count - 1, 0)) * 0.5).astype(BF16).astype(F32)
    quarter = ((half + pltpu.roll(half, count - 2, 0)) * 0.5).astype(BF16).astype(F32)
    chunks = chans // LANES
    cols = width // 4
    for chunk in range(chunks):
        wide_ref[chunk] = quarter[:, chunk * LANES : (chunk + 1) * LANES]
    source = lax.broadcasted_iota(jnp.int32, (4 * LANES, 4 * LANES), 0)
    target = lax.broadcasted_iota(jnp.int32, (4 * LANES, 4 * LANES), 1)
    r = source // LANES
    place = (target == 4 * (source % LANES) + 2 * (r % 2) + r // 2).astype(F32).astype(BF16)
    for out_row in range(rows // 4):
        for chunk in range(chunks):
            for sub in range(4):
                start = (4 * out_row + sub) * width
                packed_ref[chunk * cols : (chunk + 1) * cols, sub * LANES : (sub + 1) * LANES] = wide_ref[
                    chunk, pl.ds(start, cols, stride=4), :
                ]
        spread = jnp.dot(packed_ref[...].astype(BF16), place, preferred_element_type=F32)
        for chunk in range(chunks):
            latent_ref[out_row, :, chunk * 4 * LANES : (chunk + 1) * 4 * LANES] = spread[
                chunk * cols : (chunk + 1) * cols
            ].astype(BF16)


def image_stage(flags, inner, outer, pixels, weight_first, weight_second):
    rows, width, chans = pixels.shape
    flops = 2 * 9 * width * chans * chans * (2 * rows + 2)
    moved = 2 * (weight_first.size + weight_second.size + 3 * pixels.size)
    return pl.pallas_call(
        image_kernel,
        out_shape=jax.ShapeDtypeStruct((rows // 4, width // 4, 4 * chans), BF16),
        in_specs=[VMEM] * 6,
        out_specs=VMEM,
        scratch_shapes=[
            pltpu.VMEM((chans // LANES, rows * width, LANES), F32),
            pltpu.VMEM((chans // LANES * (width // 4), 4 * LANES), F32),
        ],
        compiler_params=pltpu.CompilerParams(vmem_limit_bytes=20 << 20),
        cost_estimate=pl.CostEstimate(flops=flops, bytes_accessed=moved, transcendentals=rows * width * chans),
        name="image_stage",
    )(flags, inner, outer, pixels, weight_first, weight_second)


def shift_rows(value, step, block, cols):
    if step == 0:
        return value
    pieces = [value[LOW_ORDER[u] * block : (LOW_ORDER[u] + 1) * block] for u in range(LOW)]
    high = lax.broadcasted_iota(jnp.int32, pieces[0].shape, 0) // cols
    if step > 0:
        wrapped = jnp.where(high < block // cols - 1, pltpu.roll(pieces[0], block - cols, 0), 0.0)
        pieces = pieces[1:] + [wrapped]
    else:
        wrapped = jnp.where(high > 0, pltpu.roll(pieces[-1], cols, 0), 0.0)
        pieces = [wrapped] + pieces[:-1]
    return jnp.concatenate([pieces[u] for u in LOW_ORDER], axis=0)


SPOTS = [(side, place) for side in range(LOW // 2) for place in range(LINE)]


def block_of(value, core, side, place, cols):
    start = ((core * (LOW // 2) + side) * LINE + place) * cols
    return value[start : start + cols]


def halve(total, flags, inner, keep_ref, *send_refs):
    width = len(send_refs) + 1
    for run in range(total.shape[0] // (width * inner)):
        parts = [total[(width * run + k) * inner : (width * run + k + 1) * inner] for k in range(width)]
        for bit, flag in enumerate(flags):
            parts = [jnp.where(flag, parts[k ^ (1 << bit)], parts[k]) for k in range(width)]
        keep_ref[run * inner : (run + 1) * inner] = parts[0]
        for part, send_ref in zip(parts[1:], send_refs):
            send_ref[run * inner : (run + 1) * inner] = part.astype(send_ref.dtype)


def latent_kernel(cols, flags_ref, gathered_ref, mix_ref, out_ref, keep_ref, send_ref):
    feature = gathered_ref[...]
    block = feature.shape[0] // LOW
    hidden_count = mix_ref.shape[3]
    taps = [(a, b) for a in range(3) for b in range(3)]
    terms = {}
    for start in range(0, 9, 2):
        pair = taps[start : start + 2]
        weight = jnp.concatenate([mix_ref[a, b] for a, b in pair], axis=1)
        both = jnp.dot(feature, weight, preferred_element_type=F32)
        for slot, tap in enumerate(pair):
            terms[tap] = both[:, slot * hidden_count : (slot + 1) * hidden_count]
    summed = None
    for a in range(3):
        line = terms[a, 1] + shift_cols(terms[a, 0], -1, cols) + shift_cols(terms[a, 2], 1, cols)
        line = shift_rows(line, a - 1, block, cols)
        summed = line if summed is None else summed + line
    hidden = silu(summed).astype(BF16).astype(F32)
    moved = []
    for a in range(3):
        line = shift_rows(hidden, a - 1, block, cols)
        for b in range(3):
            moved.append(shift_cols(line, b - 1, cols).astype(BF16))
    stacked = jnp.concatenate(moved, axis=1)
    weight = out_ref[...].reshape(9 * hidden_count, out_ref.shape[3])
    total = jnp.dot(stacked, weight, preferred_element_type=F32)
    kind = flag_of(flags_ref, flags_ref.shape[0] - 1)
    for index, (side, place) in enumerate(SPOTS):
        first, second = [block_of(total, kind_of(which, side, place), side, place, cols) for which in range(2)]
        keep_ref[index * cols : (index + 1) * cols] = pick(kind, second, first)
        send_ref[index * cols : (index + 1) * cols] = pick(kind, first, second).astype(send_ref.dtype)


def latent_stage(flags, gathered, weight_mix, weight_out, cols):
    count, chans = gathered.shape
    flops = 2 * count * (weight_mix.size + weight_out.size)
    moved = 2 * (weight_mix.size + weight_out.size) + 6 * gathered.size
    return pl.pallas_call(
        functools.partial(latent_kernel, cols),
        out_shape=[jax.ShapeDtypeStruct((count // 2, chans), kind) for kind in (F32, BF16)],
        in_specs=[VMEM] * 4,
        out_specs=[VMEM] * 2,
        compiler_params=pltpu.CompilerParams(vmem_limit_bytes=20 << 20),
        cost_estimate=pl.CostEstimate(flops=flops, bytes_accessed=moved, transcendentals=count * weight_mix.shape[3]),
        name="latent_stage",
    )(flags, gathered, weight_mix, weight_out)


def swap(value, peers, bit):
    return lax.ppermute(value, "rows", [(i, i ^ bit) for i in range(peers)])


def halo(value, peers):
    pairs = [(i, i + 1) for i in range(0, peers - 1, 2)], [(i, i + 1) for i in range(1, peers - 1, 2)]
    both = [one + [(j, i) for i, j in one] for one in pairs]
    outer = lax.ppermute(value, "rows", both[1])
    inner = lax.ppermute(value, "rows", both[0])
    return inner, outer


def merge_kernel(index, inner, flags_ref, *refs):
    *blocks, both_ref = refs
    width = len(blocks)
    flags = [flag_of(flags_ref, index + bit) for bit in range((width - 1).bit_length())]
    values = [ref[...].astype(F32) for ref in blocks]
    for block in range(values[0].shape[0] // inner):
        parts = [value[block * inner : (block + 1) * inner] for value in values]
        for bit, flag in enumerate(flags):
            parts = [jnp.where(flag, parts[k ^ (1 << bit)], parts[k]) for k in range(width)]
        for k, part in enumerate(parts):
            start = (width * block + k) * inner
            both_ref[start : start + inner] = part.astype(both_ref.dtype)


def unite_kernel(flags_ref, own_ref, got_ref, both_ref):
    kind = flag_of(flags_ref, flags_ref.shape[0] - 1)
    own, got = own_ref[...].astype(F32), got_ref[...].astype(F32)
    kinds = [pick(kind, got, own), pick(kind, own, got)]
    cols = own.shape[0] // len(SPOTS)
    for index, (side, place) in enumerate(SPOTS):
        for core in range(2):
            start = ((core * (LOW // 2) + side) * LINE + place) * cols
            block = kinds[kind_of(core, side, place)][index * cols : (index + 1) * cols]
            both_ref[start : start + cols] = block.astype(both_ref.dtype)


def united(flags, own, got):
    rows, chans = own.shape
    return pl.pallas_call(
        unite_kernel,
        out_shape=jax.ShapeDtypeStruct((2 * rows, chans), own.dtype),
        in_specs=[VMEM] * 3,
        out_specs=VMEM,
        compiler_params=pltpu.CompilerParams(vmem_limit_bytes=2 << 20),
        cost_estimate=pl.CostEstimate(flops=0, bytes_accessed=8 * own.size, transcendentals=0),
        name="unite",
    )(flags, own, got)


def merged(flags, blocks, index, inner, cover=0):
    rows, chans = blocks[0].shape
    return pl.pallas_call(
        functools.partial(merge_kernel, index, inner),
        out_shape=jax.ShapeDtypeStruct((len(blocks) * rows, chans), blocks[0].dtype),
        in_specs=[VMEM] * (1 + len(blocks)),
        out_specs=VMEM,
        compiler_params=pltpu.CompilerParams(vmem_limit_bytes=2 << 20),
        cost_estimate=pl.CostEstimate(flops=cover, bytes_accessed=8 * blocks[0].size, transcendentals=0),
        name="merge",
    )(flags, *blocks)


def exchanged(values, peers):
    got = []
    for k, value in enumerate(values, 1):
        got.append(swap(value, peers, LOW * k + kind_of(0, 0, k)))
    return got


def gather_rows(latent, flags, peers, cols):
    held = merged(flags, [latent, *exchanged([latent] * (LINE - 1), peers)], LOW.bit_length() - 1, cols, COVER)
    held = merged(flags, [held, swap(held, peers, 2 + SIDE_FLIP)], 1, held.shape[0])
    return united(flags, held, swap(held, peers, 1))


def halve_kernel(index, inner, flags_ref, held_ref, got_ref, keep_ref, *send_refs):
    flags = [flag_of(flags_ref, index + bit) for bit in range(len(send_refs).bit_length())]
    halve(held_ref[...] + got_ref[...].astype(F32), flags, inner, keep_ref, *send_refs)


def halved(flags, held, got, index, inner, width=2):
    shape = (held.shape[0] // width, held.shape[1])
    keep, *sends = pl.pallas_call(
        functools.partial(halve_kernel, index, inner),
        out_shape=[jax.ShapeDtypeStruct(shape, kind) for kind in [F32] + [BF16] * (width - 1)],
        in_specs=[VMEM] * 3,
        out_specs=[VMEM] * width,
        compiler_params=pltpu.CompilerParams(vmem_limit_bytes=2 << 20),
        cost_estimate=pl.CostEstimate(flops=held.size, bytes_accessed=6 * held.size, transcendentals=0),
        name="halve",
    )(flags, held, got)
    return keep, sends


def scatter_sum(keep, send, flags, peers, cols):
    got = swap(send, peers, 1)
    keep, sends = halved(flags, keep, got, 1, LINE * cols)
    got = swap(sends[0], peers, 2 + SIDE_FLIP)
    keep, sends = halved(flags, keep, got, LOW.bit_length() - 1, cols, LINE)
    for got in exchanged(sends, peers):
        keep = keep + got.astype(F32)
    return keep


def plain_latent(latent, weight_mix, weight_out):
    whole = lax.all_gather(latent, "rows", axis=0, tiled=True)

    def conv(value, weight):
        rows, cols = value.shape[:2]
        padded = jnp.pad(value, ((1, 1), (1, 1), (0, 0)))
        summed = 0.0
        for a in range(3):
            for b in range(3):
                summed = summed + jnp.dot(
                    padded[a : a + rows, b : b + cols], weight[a, b], preferred_element_type=F32
                )
        return summed

    hidden = jax.nn.silu(conv(whole, weight_mix)).astype(BF16)
    mixed = lax.psum_scatter(conv(hidden, weight_out), "rows", scatter_dimension=0, tiled=True)
    return (latent.astype(F32) + mixed).astype(BF16)


def compute(pixels, weight_first, weight_second, weight_mix, weight_out):
    peers = lax.axis_size("rows")
    me = lax.axis_index("rows")
    flags = placed(me, peers)
    inner, outer = halo(pixels, peers)
    latent = image_stage(flags, inner, outer, pixels, weight_first, weight_second)
    if peers != LINE * LOW or latent.shape[0] != 1 or weight_mix.shape[3] % LANES:
        return plain_latent(latent, weight_mix, weight_out)
    cols = latent.shape[1]
    gathered = gather_rows(latent[0], flags, peers, cols)
    keep, send = latent_stage(flags, gathered, weight_mix, weight_out, cols)
    mixed = scatter_sum(keep, send, flags, peers, cols)
    return (latent.astype(F32) + mixed[None]).astype(BF16)


def solution(mesh):
    return jax.shard_map(
        compute,
        mesh=mesh,
        in_specs=(
            P(("groups", "rows"), None, None),
            P(),
            P(),
            P(None, None, None, "rows"),
            P(None, None, "rows", None),
        ),
        out_specs=P(("groups", "rows"), None, None),
        check_vma=False,
    )
```

```python
import functools

import jax
import jax.numpy as jnp
from jax import lax
from jax.experimental import pallas as pl
from jax.experimental.pallas import tpu as pltpu
from jax.sharding import PartitionSpec as P


F32 = jnp.float32
BF16 = jnp.bfloat16
LOW = 4
LOW_ORDER = (0, 2, 1, 3)
LINE = 4
NEAR_FLIP, FAR_FLIP, SIDE_FLIP = 0, 1, 1
LANES = 128
VMEM = pl.BlockSpec(memory_space=pltpu.VMEM)
COVER = 2 * 10**10


def silu(value):
    return value / (1.0 + jnp.exp(-value))


def flag_of(flags_ref, index):
    return flags_ref[index, :1, :1] != 0


def pick(flag, one, other):
    return jnp.where(flag, one.astype(F32), other.astype(F32))


def kind_of(core, side, place):
    return core ^ (SIDE_FLIP * side) ^ (NEAR_FLIP * (place & 1)) ^ (FAR_FLIP * (place >> 1))


def place_kernel(bits, last, me_ref, flags_ref):
    me = me_ref[...]
    for bit in range(bits):
        flags_ref[bit] = (me >> bit) & 1
    flags_ref[bits] = (me == 0).astype(jnp.int32)
    flags_ref[bits + 1] = (me == last).astype(jnp.int32)
    flags_ref[bits + 2] = kind_of(me & 1, (me >> 1) & 1, (me >> 2) & 3)


def placed(me, peers):
    bits = max(1, (peers - 1).bit_length())
    return pl.pallas_call(
        functools.partial(place_kernel, bits, peers - 1),
        out_shape=jax.ShapeDtypeStruct((bits + 3, 8, LANES), jnp.int32),
        in_specs=[VMEM],
        out_specs=VMEM,
        compiler_params=pltpu.CompilerParams(vmem_limit_bytes=2 << 20),
        cost_estimate=pl.CostEstimate(flops=COVER, bytes_accessed=0, transcendentals=0),
        name="place",
    )(jnp.broadcast_to(me, (8, LANES)))


def shift_cols(value, step, width):
    if step == 0:
        return value
    count = value.shape[0]
    moved = pltpu.roll(value, (-step) % count, 0)
    col = lax.broadcasted_iota(jnp.int32, value.shape, 0) % width
    keep = (col + step >= 0) & (col + step < width)
    return jnp.where(keep, moved, 0.0)


def conv_image(feature, weight_ref, width):
    out_rows = feature.shape[0] - 2 * width
    total = None
    for col_tap in (1, 0, 2):
        term = None
        for row_tap in range(3):
            part = jnp.dot(
                feature[row_tap * width : row_tap * width + out_rows],
                weight_ref[row_tap, col_tap],
                preferred_element_type=F32,
            )
            term = part if term is None else term + part
        term = shift_cols(term, col_tap - 1, width)
        total = term if total is None else total + term
    return total


def image_kernel(flags_ref, inner_ref, outer_ref, pixels_ref, first_ref, second_ref, latent_ref, wide_ref, packed_ref):
    rows, width, chans = pixels_ref.shape
    flat = lambda ref: ref[...].reshape(ref.shape[0] * width, chans)
    pixels = flat(pixels_ref)
    odd, bits = flag_of(flags_ref, 0), flags_ref.shape[0] - 3
    inner, outer = flat(inner_ref), flat(outer_ref)
    edge = 2 * width
    before = pick(odd, inner[-edge:], outer[-edge:]).astype(BF16)
    after = pick(odd, outer[:edge], inner[:edge]).astype(BF16)
    before = jnp.where(flag_of(flags_ref, bits), 0.0, before.astype(F32)).astype(BF16)
    after = jnp.where(flag_of(flags_ref, bits + 1), 0.0, after.astype(F32)).astype(BF16)
    extended = jnp.concatenate([before, pixels, after], axis=0)
    activated = silu(conv_image(extended, first_ref, width)).astype(BF16).astype(F32)
    row = lax.broadcasted_iota(jnp.int32, activated.shape, 0) // width
    inside = (row >= flags_ref[bits, :1, :1]) & (row < rows + 2 - flags_ref[bits + 1, :1, :1])
    activated = jnp.where(inside, activated, 0.0).astype(BF16)
    block = pixels.astype(F32) + conv_image(activated, second_ref, width)
    block = block.astype(BF16).astype(F32)
    count = rows * width
    half = ((block + pltpu.roll(block, count - 1, 0)) * 0.5).astype(BF16).astype(F32)
    quarter = ((half + pltpu.roll(half, count - 2, 0)) * 0.5).astype(BF16).astype(F32)
    chunks = chans // LANES
    cols = width // 4
    for chunk in range(chunks):
        wide_ref[chunk] = quarter[:, chunk * LANES : (chunk + 1) * LANES]
    source = lax.broadcasted_iota(jnp.int32, (4 * LANES, 4 * LANES), 0)
    target = lax.broadcasted_iota(jnp.int32, (4 * LANES, 4 * LANES), 1)
    r = source // LANES
    place = (target == 4 * (source % LANES) + 2 * (r % 2) + r // 2).astype(F32).astype(BF16)
    for out_row in range(rows // 4):
        for chunk in range(chunks):
            for sub in range(4):
                start = (4 * out_row + sub) * width
                packed_ref[chunk * cols : (chunk + 1) * cols, sub * LANES : (sub + 1) * LANES] = wide_ref[
                    chunk, pl.ds(start, cols, stride=4), :
                ]
        spread = jnp.dot(packed_ref[...].astype(BF16), place, preferred_element_type=F32)
        for chunk in range(chunks):
            latent_ref[out_row, :, chunk * 4 * LANES : (chunk + 1) * 4 * LANES] = spread[
                chunk * cols : (chunk + 1) * cols
            ].astype(BF16)


def image_stage(flags, inner, outer, pixels, weight_first, weight_second):
    rows, width, chans = pixels.shape
    flops = 2 * 9 * width * chans * chans * (2 * rows + 2)
    moved = 2 * (weight_first.size + weight_second.size + 3 * pixels.size)
    return pl.pallas_call(
        image_kernel,
        out_shape=jax.ShapeDtypeStruct((rows // 4, width // 4, 4 * chans), BF16),
        in_specs=[VMEM] * 6,
        out_specs=VMEM,
        scratch_shapes=[
            pltpu.VMEM((chans // LANES, rows * width, LANES), F32),
            pltpu.VMEM((chans // LANES * (width // 4), 4 * LANES), F32),
        ],
        compiler_params=pltpu.CompilerParams(vmem_limit_bytes=20 << 20),
        cost_estimate=pl.CostEstimate(flops=flops, bytes_accessed=moved, transcendentals=rows * width * chans),
        name="image_stage",
    )(flags, inner, outer, pixels, weight_first, weight_second)


def shift_rows(value, step, block, cols):
    if step == 0:
        return value
    pieces = [value[LOW_ORDER[u] * block : (LOW_ORDER[u] + 1) * block] for u in range(LOW)]
    high = lax.broadcasted_iota(jnp.int32, pieces[0].shape, 0) // cols
    if step > 0:
        wrapped = jnp.where(high < block // cols - 1, pltpu.roll(pieces[0], block - cols, 0), 0.0)
        pieces = pieces[1:] + [wrapped]
    else:
        wrapped = jnp.where(high > 0, pltpu.roll(pieces[-1], cols, 0), 0.0)
        pieces = [wrapped] + pieces[:-1]
    return jnp.concatenate([pieces[u] for u in LOW_ORDER], axis=0)


SPOTS = [(side, place) for side in range(LOW // 2) for place in range(LINE)]


def block_of(value, core, side, place, cols):
    start = ((core * (LOW // 2) + side) * LINE + place) * cols
    return value[start : start + cols]


def halve(total, flags, inner, keep_ref, *send_refs):
    width = len(send_refs) + 1
    for run in range(total.shape[0] // (width * inner)):
        parts = [total[(width * run + k) * inner : (width * run + k + 1) * inner] for k in range(width)]
        for bit, flag in enumerate(flags):
            parts = [jnp.where(flag, parts[k ^ (1 << bit)], parts[k]) for k in range(width)]
        keep_ref[run * inner : (run + 1) * inner] = parts[0]
        for part, send_ref in zip(parts[1:], send_refs):
            send_ref[run * inner : (run + 1) * inner] = part.astype(send_ref.dtype)


def latent_kernel(cols, flags_ref, gathered_ref, mix_ref, out_ref, keep_ref, send_ref):
    feature = gathered_ref[...]
    block = feature.shape[0] // LOW
    hidden_count = mix_ref.shape[3]
    taps = [(a, b) for a in range(3) for b in range(3)]
    terms = {}
    for start in range(0, 9, 2):
        pair = taps[start : start + 2]
        weight = jnp.concatenate([mix_ref[a, b] for a, b in pair], axis=1)
        both = jnp.dot(feature, weight, preferred_element_type=F32)
        for slot, tap in enumerate(pair):
            terms[tap] = both[:, slot * hidden_count : (slot + 1) * hidden_count]
    summed = None
    for a in range(3):
        line = terms[a, 1] + shift_cols(terms[a, 0], -1, cols) + shift_cols(terms[a, 2], 1, cols)
        line = shift_rows(line, a - 1, block, cols)
        summed = line if summed is None else summed + line
    hidden = silu(summed).astype(BF16).astype(F32)
    moved = []
    for a in range(3):
        line = shift_rows(hidden, a - 1, block, cols)
        for b in range(3):
            moved.append(shift_cols(line, b - 1, cols).astype(BF16))
    stacked = jnp.concatenate(moved, axis=1)
    weight = out_ref[...].reshape(9 * hidden_count, out_ref.shape[3])
    total = jnp.dot(stacked, weight, preferred_element_type=F32)
    kind = flag_of(flags_ref, flags_ref.shape[0] - 1)
    for index, (side, place) in enumerate(SPOTS):
        first, second = [block_of(total, kind_of(which, side, place), side, place, cols) for which in range(2)]
        keep_ref[index * cols : (index + 1) * cols] = pick(kind, second, first)
        send_ref[index * cols : (index + 1) * cols] = pick(kind, first, second).astype(send_ref.dtype)


def latent_stage(flags, gathered, weight_mix, weight_out, cols):
    count, chans = gathered.shape
    flops = 2 * count * (weight_mix.size + weight_out.size)
    moved = 2 * (weight_mix.size + weight_out.size) + 6 * gathered.size
    return pl.pallas_call(
        functools.partial(latent_kernel, cols),
        out_shape=[jax.ShapeDtypeStruct((count // 2, chans), kind) for kind in (F32, BF16)],
        in_specs=[VMEM] * 4,
        out_specs=[VMEM] * 2,
        compiler_params=pltpu.CompilerParams(vmem_limit_bytes=20 << 20),
        cost_estimate=pl.CostEstimate(flops=flops, bytes_accessed=moved, transcendentals=count * weight_mix.shape[3]),
        name="latent_stage",
    )(flags, gathered, weight_mix, weight_out)


def swap(value, peers, bit):
    return lax.ppermute(value, "rows", [(i, i ^ bit) for i in range(peers)])


def halo(value, peers, groups):
    got = []
    for first in (0, 1):
        partner = {}
        for i in range(first, peers - 1, 2):
            partner[i], partner[i + 1] = i + 1, i
        pairs = []
        for group in range(groups):
            for i in range(peers):
                if i in partner:
                    pairs.append((group * peers + i, group * peers + partner[i]))
                elif group ^ 1 < groups:
                    pairs.append((group * peers + i, (group ^ 1) * peers + i))
        got.append(lax.ppermute(value, ("groups", "rows"), pairs))
    return got


def merge_kernel(index, inner, flags_ref, *refs):
    *blocks, both_ref = refs
    width = len(blocks)
    flags = [flag_of(flags_ref, index + bit) for bit in range((width - 1).bit_length())]
    values = [ref[...].astype(F32) for ref in blocks]
    for block in range(values[0].shape[0] // inner):
        parts = [value[block * inner : (block + 1) * inner] for value in values]
        for bit, flag in enumerate(flags):
            parts = [jnp.where(flag, parts[k ^ (1 << bit)], parts[k]) for k in range(width)]
        for k, part in enumerate(parts):
            start = (width * block + k) * inner
            both_ref[start : start + inner] = part.astype(both_ref.dtype)


def unite_kernel(flags_ref, own_ref, got_ref, both_ref):
    kind = flag_of(flags_ref, flags_ref.shape[0] - 1)
    own, got = own_ref[...].astype(F32), got_ref[...].astype(F32)
    kinds = [pick(kind, got, own), pick(kind, own, got)]
    cols = own.shape[0] // len(SPOTS)
    for index, (side, place) in enumerate(SPOTS):
        for core in range(2):
            start = ((core * (LOW // 2) + side) * LINE + place) * cols
            block = kinds[kind_of(core, side, place)][index * cols : (index + 1) * cols]
            both_ref[start : start + cols] = block.astype(both_ref.dtype)


def united(flags, own, got):
    rows, chans = own.shape
    return pl.pallas_call(
        unite_kernel,
        out_shape=jax.ShapeDtypeStruct((2 * rows, chans), own.dtype),
        in_specs=[VMEM] * 3,
        out_specs=VMEM,
        compiler_params=pltpu.CompilerParams(vmem_limit_bytes=2 << 20),
        cost_estimate=pl.CostEstimate(flops=0, bytes_accessed=8 * own.size, transcendentals=0),
        name="unite",
    )(flags, own, got)


def merged(flags, blocks, index, inner, cover=0):
    rows, chans = blocks[0].shape
    return pl.pallas_call(
        functools.partial(merge_kernel, index, inner),
        out_shape=jax.ShapeDtypeStruct((len(blocks) * rows, chans), blocks[0].dtype),
        in_specs=[VMEM] * (1 + len(blocks)),
        out_specs=VMEM,
        compiler_params=pltpu.CompilerParams(vmem_limit_bytes=2 << 20),
        cost_estimate=pl.CostEstimate(flops=cover, bytes_accessed=8 * blocks[0].size, transcendentals=0),
        name="merge",
    )(flags, *blocks)


def exchanged(values, peers):
    got = []
    for k, value in enumerate(values, 1):
        got.append(swap(value, peers, LOW * k + kind_of(0, 0, k)))
    return got


def gather_rows(latent, flags, peers, cols):
    held = merged(flags, [latent, *exchanged([latent] * (LINE - 1), peers)], LOW.bit_length() - 1, cols, COVER)
    held = merged(flags, [held, swap(held, peers, 2 + SIDE_FLIP)], 1, held.shape[0])
    return united(flags, held, swap(held, peers, 1))


def halve_kernel(index, inner, flags_ref, held_ref, got_ref, keep_ref, *send_refs):
    flags = [flag_of(flags_ref, index + bit) for bit in range(len(send_refs).bit_length())]
    halve(held_ref[...] + got_ref[...].astype(F32), flags, inner, keep_ref, *send_refs)


def halved(flags, held, got, index, inner, width=2):
    shape = (held.shape[0] // width, held.shape[1])
    keep, *sends = pl.pallas_call(
        functools.partial(halve_kernel, index, inner),
        out_shape=[jax.ShapeDtypeStruct(shape, kind) for kind in [F32] + [BF16] * (width - 1)],
        in_specs=[VMEM] * 3,
        out_specs=[VMEM] * width,
        compiler_params=pltpu.CompilerParams(vmem_limit_bytes=2 << 20),
        cost_estimate=pl.CostEstimate(flops=held.size, bytes_accessed=6 * held.size, transcendentals=0),
        name="halve",
    )(flags, held, got)
    return keep, sends


def scatter_sum(keep, send, flags, peers, cols):
    got = swap(send, peers, 1)
    keep, sends = halved(flags, keep, got, 1, LINE * cols)
    got = swap(sends[0], peers, 2 + SIDE_FLIP)
    keep, sends = halved(flags, keep, got, LOW.bit_length() - 1, cols, LINE)
    for got in exchanged(sends, peers):
        keep = keep + got.astype(F32)
    return keep


def plain_latent(latent, weight_mix, weight_out):
    whole = lax.all_gather(latent, "rows", axis=0, tiled=True)

    def conv(value, weight):
        rows, cols = value.shape[:2]
        padded = jnp.pad(value, ((1, 1), (1, 1), (0, 0)))
        summed = 0.0
        for a in range(3):
            for b in range(3):
                summed = summed + jnp.dot(
                    padded[a : a + rows, b : b + cols], weight[a, b], preferred_element_type=F32
                )
        return summed

    hidden = jax.nn.silu(conv(whole, weight_mix)).astype(BF16)
    mixed = lax.psum_scatter(conv(hidden, weight_out), "rows", scatter_dimension=0, tiled=True)
    return (latent.astype(F32) + mixed).astype(BF16)


def compute(pixels, weight_first, weight_second, weight_mix, weight_out):
    peers = lax.axis_size("rows")
    me = lax.axis_index("rows")
    flags = placed(me, peers)
    inner, outer = halo(pixels, peers, lax.axis_size("groups"))
    latent = image_stage(flags, inner, outer, pixels, weight_first, weight_second)
    if peers != LINE * LOW or latent.shape[0] != 1 or weight_mix.shape[3] % LANES:
        return plain_latent(latent, weight_mix, weight_out)
    cols = latent.shape[1]
    gathered = gather_rows(latent[0], flags, peers, cols)
    keep, send = latent_stage(flags, gathered, weight_mix, weight_out, cols)
    mixed = scatter_sum(keep, send, flags, peers, cols)
    return (latent.astype(F32) + mixed[None]).astype(BF16)


def solution(mesh):
    return jax.shard_map(
        compute,
        mesh=mesh,
        in_specs=(
            P(("groups", "rows"), None, None),
            P(),
            P(),
            P(None, None, None, "rows"),
            P(None, None, "rows", None),
        ),
        out_specs=P(("groups", "rows"), None, None),
        check_vma=False,
    )
```

```python
import functools

import jax
import jax.numpy as jnp
from jax import lax
from jax.experimental import pallas as pl
from jax.experimental.pallas import tpu as pltpu
from jax.sharding import PartitionSpec as P


F32 = jnp.float32
BF16 = jnp.bfloat16
LOW = 4
LOW_ORDER = (0, 2, 1, 3)
LINE = 4
NEAR_FLIP, FAR_FLIP, SIDE_FLIP = 0, 1, 1
LANES = 128
VMEM = pl.BlockSpec(memory_space=pltpu.VMEM)
COVER = 2 * 10**10


def silu(value):
    return value / (1.0 + jnp.exp(-value))


def flag_of(flags_ref, index):
    return flags_ref[index, :1, :1] != 0


def pick(flag, one, other):
    return jnp.where(flag, one.astype(F32), other.astype(F32))


def kind_of(core, side, place):
    return core ^ (SIDE_FLIP * side) ^ (NEAR_FLIP * (place & 1)) ^ (FAR_FLIP * (place >> 1))


def place_kernel(bits, last, me_ref, flags_ref, spread_ref):
    me = me_ref[...]
    for bit in range(bits):
        flags_ref[bit] = (me >> bit) & 1
    flags_ref[bits] = (me == 0).astype(jnp.int32)
    flags_ref[bits + 1] = (me == last).astype(jnp.int32)
    flags_ref[bits + 2] = kind_of(me & 1, (me >> 1) & 1, (me >> 2) & 3)
    shape = (LANES, spread_ref.shape[1])
    source = lax.broadcasted_iota(jnp.int32, shape, 0)
    target = lax.broadcasted_iota(jnp.int32, shape, 1)
    for r in range(4):
        place = target == 4 * source + 2 * (r % 2) + r // 2
        spread_ref[r * LANES : (r + 1) * LANES] = place.astype(F32).astype(spread_ref.dtype)


def placed(me, peers):
    bits = max(1, (peers - 1).bit_length())
    return pl.pallas_call(
        functools.partial(place_kernel, bits, peers - 1),
        out_shape=[
            jax.ShapeDtypeStruct((bits + 3, 8, LANES), jnp.int32),
            jax.ShapeDtypeStruct((4 * LANES, 4 * LANES), BF16),
        ],
        in_specs=[VMEM],
        out_specs=[VMEM] * 2,
        compiler_params=pltpu.CompilerParams(vmem_limit_bytes=2 << 20),
        cost_estimate=pl.CostEstimate(flops=COVER, bytes_accessed=0, transcendentals=0),
        name="place",
    )(jnp.broadcast_to(me, (8, LANES)))


def shift_cols(value, step, width):
    if step == 0:
        return value
    count = value.shape[0]
    moved = pltpu.roll(value, (-step) % count, 0)
    col = lax.broadcasted_iota(jnp.int32, value.shape, 0) % width
    keep = (col + step >= 0) & (col + step < width)
    return jnp.where(keep, moved, 0.0)


def conv_image(feature, weight_ref, width):
    out_rows = feature.shape[0] - 2 * width
    total = None
    for col_tap in (0, 2, 1):
        term = None
        for row_tap in range(3):
            part = jnp.dot(
                feature[row_tap * width : row_tap * width + out_rows],
                weight_ref[row_tap, col_tap],
                preferred_element_type=F32,
            )
            term = part if term is None else term + part
        term = shift_cols(term, col_tap - 1, width)
        total = term if total is None else total + term
    return total


def averaged(value_ref, chunk, count):
    first, second = value_ref[chunk, pl.ds(0, count, stride=2), :], value_ref[chunk, pl.ds(1, count, stride=2), :]
    return ((first + second) * 0.5).astype(BF16).astype(F32)


def first_kernel(flags_ref, inner_ref, outer_ref, pixels_ref, first_ref, activated_ref):
    rows, width, chans = pixels_ref.shape
    flat = lambda ref: ref[...].reshape(ref.shape[0] * width, chans)
    pixels = flat(pixels_ref)
    odd, bits = flag_of(flags_ref, 0), flags_ref.shape[0] - 3
    inner, outer = flat(inner_ref), flat(outer_ref)
    edge = 2 * width
    before = pick(odd, inner[-edge:], outer[-edge:]).astype(BF16)
    after = pick(odd, outer[:edge], inner[:edge]).astype(BF16)
    before = jnp.where(flag_of(flags_ref, bits), 0.0, before.astype(F32)).astype(BF16)
    after = jnp.where(flag_of(flags_ref, bits + 1), 0.0, after.astype(F32)).astype(BF16)
    extended = jnp.concatenate([before, pixels, after], axis=0)
    activated = silu(conv_image(extended, first_ref, width)).astype(BF16).astype(F32)
    row = lax.broadcasted_iota(jnp.int32, activated.shape, 0) // width
    inside = (row >= flags_ref[bits, :1, :1]) & (row < rows + 2 - flags_ref[bits + 1, :1, :1])
    activated_ref[...] = jnp.where(inside, activated, 0.0).astype(BF16)


def second_kernel(activated_ref, pixels_ref, spread_ref, second_ref, latent_ref, wide_ref, half_ref, packed_ref):
    rows, width, chans = pixels_ref.shape
    pixels = pixels_ref[...].reshape(rows * width, chans)
    block = pixels.astype(F32) + conv_image(activated_ref[...], second_ref, width)
    block = block.astype(BF16).astype(F32)
    count = rows * width
    chunks = chans // LANES
    cols = width // 4
    for chunk in range(chunks):
        wide_ref[chunk] = block[:, chunk * LANES : (chunk + 1) * LANES]
    for chunk in range(chunks):
        half_ref[chunk] = averaged(wide_ref, chunk, count // 2)
    quarters = [averaged(half_ref, chunk, count // 4) for chunk in range(chunks)]
    for out_row in range(rows // 4):
        for chunk in range(chunks):
            for sub in range(4):
                start = (4 * out_row + sub) * cols
                packed_ref[chunk * cols : (chunk + 1) * cols, sub * LANES : (sub + 1) * LANES] = quarters[chunk][
                    start : start + cols
                ]
        latent = jnp.dot(packed_ref[...].astype(BF16), spread_ref[...], preferred_element_type=F32)
        for chunk in range(chunks):
            latent_ref[out_row, :, chunk * 4 * LANES : (chunk + 1) * 4 * LANES] = latent[
                chunk * cols : (chunk + 1) * cols
            ].astype(BF16)


def image_stage(flags, spread, inner, outer, pixels, weight_first, weight_second):
    rows, width, chans = pixels.shape
    cost = lambda count, weight: pl.CostEstimate(
        flops=2 * count * weight.size, bytes_accessed=2 * weight.size + 6 * pixels.size, transcendentals=0
    )
    activated = pl.pallas_call(
        first_kernel,
        out_shape=jax.ShapeDtypeStruct(((rows + 2) * width, chans), BF16),
        in_specs=[VMEM] * 5,
        out_specs=VMEM,
        compiler_params=pltpu.CompilerParams(vmem_limit_bytes=16 << 20),
        cost_estimate=cost((rows + 2) * width, weight_first),
        name="first_stage",
    )(flags, inner, outer, pixels, weight_first)
    return pl.pallas_call(
        second_kernel,
        out_shape=jax.ShapeDtypeStruct((rows // 4, width // 4, 4 * chans), BF16),
        in_specs=[VMEM] * 4,
        out_specs=VMEM,
        scratch_shapes=[
            pltpu.VMEM((chans // LANES, rows * width, LANES), F32),
            pltpu.VMEM((chans // LANES, rows * width // 2, LANES), F32),
            pltpu.VMEM((chans // LANES * (width // 4), 4 * LANES), F32),
        ],
        compiler_params=pltpu.CompilerParams(vmem_limit_bytes=16 << 20),
        cost_estimate=cost(rows * width, weight_second),
        name="image_stage",
    )(activated, pixels, spread, weight_second)


def shift_rows(value, step, block, cols):
    if step == 0:
        return value
    pieces = [value[LOW_ORDER[u] * block : (LOW_ORDER[u] + 1) * block] for u in range(LOW)]
    high = lax.broadcasted_iota(jnp.int32, pieces[0].shape, 0) // cols
    if step > 0:
        wrapped = jnp.where(high < block // cols - 1, pltpu.roll(pieces[0], block - cols, 0), 0.0)
        pieces = pieces[1:] + [wrapped]
    else:
        wrapped = jnp.where(high > 0, pltpu.roll(pieces[-1], cols, 0), 0.0)
        pieces = [wrapped] + pieces[:-1]
    return jnp.concatenate([pieces[u] for u in LOW_ORDER], axis=0)


SPOTS = [(side, place) for side in range(LOW // 2) for place in range(LINE)]


def block_of(value, core, side, place, cols):
    start = ((core * (LOW // 2) + side) * LINE + place) * cols
    return value[start : start + cols]


def halve(total, flags, inner, keep_ref, *send_refs):
    width = len(send_refs) + 1
    for run in range(total.shape[0] // (width * inner)):
        parts = [total[(width * run + k) * inner : (width * run + k + 1) * inner] for k in range(width)]
        for bit, flag in enumerate(flags):
            parts = [jnp.where(flag, parts[k ^ (1 << bit)], parts[k]) for k in range(width)]
        keep_ref[run * inner : (run + 1) * inner] = parts[0]
        for part, send_ref in zip(parts[1:], send_refs):
            send_ref[run * inner : (run + 1) * inner] = part.astype(send_ref.dtype)


def latent_kernel(cols, flags_ref, gathered_ref, mix_ref, out_ref, keep_ref, send_ref):
    feature = gathered_ref[...]
    block = feature.shape[0] // LOW
    hidden_count = mix_ref.shape[3]
    taps = [(a, b) for a in range(3) for b in range(3)]
    terms = {}
    for start in range(0, 9, 2):
        pair = taps[start : start + 2]
        weight = jnp.concatenate([mix_ref[a, b] for a, b in pair], axis=1)
        both = jnp.dot(feature, weight, preferred_element_type=F32)
        for slot, tap in enumerate(pair):
            terms[tap] = both[:, slot * hidden_count : (slot + 1) * hidden_count]
    summed = None
    for a in range(3):
        line = terms[a, 1] + shift_cols(terms[a, 0], -1, cols) + shift_cols(terms[a, 2], 1, cols)
        line = shift_rows(line, a - 1, block, cols)
        summed = line if summed is None else summed + line
    hidden = silu(summed).astype(BF16).astype(F32)
    moved = []
    for a in range(3):
        line = shift_rows(hidden, a - 1, block, cols)
        for b in range(3):
            moved.append(shift_cols(line, b - 1, cols).astype(BF16))
    stacked = jnp.concatenate(moved, axis=1)
    weight = out_ref[...].reshape(9 * hidden_count, out_ref.shape[3])
    total = jnp.dot(stacked, weight, preferred_element_type=F32)
    kind = flag_of(flags_ref, flags_ref.shape[0] - 1)
    for index, (side, place) in enumerate(SPOTS):
        first, second = [block_of(total, kind_of(which, side, place), side, place, cols) for which in range(2)]
        keep_ref[index * cols : (index + 1) * cols] = pick(kind, second, first)
        send_ref[index * cols : (index + 1) * cols] = pick(kind, first, second).astype(send_ref.dtype)


def latent_stage(flags, gathered, weight_mix, weight_out, cols):
    count, chans = gathered.shape
    flops = 2 * count * (weight_mix.size + weight_out.size)
    moved = 2 * (weight_mix.size + weight_out.size) + 6 * gathered.size
    return pl.pallas_call(
        functools.partial(latent_kernel, cols),
        out_shape=[jax.ShapeDtypeStruct((count // 2, chans), kind) for kind in (F32, BF16)],
        in_specs=[VMEM] * 4,
        out_specs=[VMEM] * 2,
        compiler_params=pltpu.CompilerParams(vmem_limit_bytes=20 << 20),
        cost_estimate=pl.CostEstimate(flops=flops, bytes_accessed=moved, transcendentals=count * weight_mix.shape[3]),
        name="latent_stage",
    )(flags, gathered, weight_mix, weight_out)


def swap(value, peers, bit):
    return lax.ppermute(value, "rows", [(i, i ^ bit) for i in range(peers)])


def halo(value, peers, groups):
    got = []
    for first in (0, 1):
        partner = {}
        for i in range(first, peers - 1, 2):
            partner[i], partner[i + 1] = i + 1, i
        pairs = []
        for group in range(groups):
            for i in range(peers):
                if i in partner:
                    pairs.append((group * peers + i, group * peers + partner[i]))
                elif group ^ 1 < groups:
                    pairs.append((group * peers + i, (group ^ 1) * peers + i))
        got.append(lax.ppermute(value, ("groups", "rows"), pairs))
    return got


def merge_kernel(index, inner, flags_ref, *refs):
    *blocks, both_ref = refs
    width = len(blocks)
    flags = [flag_of(flags_ref, index + bit) for bit in range((width - 1).bit_length())]
    values = [ref[...].astype(F32) for ref in blocks]
    for block in range(values[0].shape[0] // inner):
        parts = [value[block * inner : (block + 1) * inner] for value in values]
        for bit, flag in enumerate(flags):
            parts = [jnp.where(flag, parts[k ^ (1 << bit)], parts[k]) for k in range(width)]
        for k, part in enumerate(parts):
            start = (width * block + k) * inner
            both_ref[start : start + inner] = part.astype(both_ref.dtype)


def unite_kernel(flags_ref, own_ref, got_ref, both_ref):
    kind = flag_of(flags_ref, flags_ref.shape[0] - 1)
    own, got = own_ref[...].astype(F32), got_ref[...].astype(F32)
    kinds = [pick(kind, got, own), pick(kind, own, got)]
    cols = own.shape[0] // len(SPOTS)
    for index, (side, place) in enumerate(SPOTS):
        for core in range(2):
            start = ((core * (LOW // 2) + side) * LINE + place) * cols
            block = kinds[kind_of(core, side, place)][index * cols : (index + 1) * cols]
            both_ref[start : start + cols] = block.astype(both_ref.dtype)


def united(flags, own, got):
    rows, chans = own.shape
    return pl.pallas_call(
        unite_kernel,
        out_shape=jax.ShapeDtypeStruct((2 * rows, chans), own.dtype),
        in_specs=[VMEM] * 3,
        out_specs=VMEM,
        compiler_params=pltpu.CompilerParams(vmem_limit_bytes=2 << 20),
        cost_estimate=pl.CostEstimate(flops=0, bytes_accessed=8 * own.size, transcendentals=0),
        name="unite",
    )(flags, own, got)


def merged(flags, blocks, index, inner, cover=0):
    rows, chans = blocks[0].shape
    return pl.pallas_call(
        functools.partial(merge_kernel, index, inner),
        out_shape=jax.ShapeDtypeStruct((len(blocks) * rows, chans), blocks[0].dtype),
        in_specs=[VMEM] * (1 + len(blocks)),
        out_specs=VMEM,
        compiler_params=pltpu.CompilerParams(vmem_limit_bytes=2 << 20),
        cost_estimate=pl.CostEstimate(flops=cover, bytes_accessed=8 * blocks[0].size, transcendentals=0),
        name="merge",
    )(flags, *blocks)


def exchanged(values, peers):
    got = []
    for k, value in enumerate(values, 1):
        got.append(swap(value, peers, LOW * k + kind_of(0, 0, k)))
    return got


def gather_rows(latent, flags, peers, cols):
    held = merged(flags, [latent, *exchanged([latent] * (LINE - 1), peers)], LOW.bit_length() - 1, cols, COVER)
    held = merged(flags, [held, swap(held, peers, 2 + SIDE_FLIP)], 1, held.shape[0])
    return united(flags, held, swap(held, peers, 1))


def halve_kernel(index, inner, flags_ref, held_ref, got_ref, keep_ref, *send_refs):
    flags = [flag_of(flags_ref, index + bit) for bit in range(len(send_refs).bit_length())]
    halve(held_ref[...] + got_ref[...].astype(F32), flags, inner, keep_ref, *send_refs)


def halved(flags, held, got, index, inner, width=2):
    shape = (held.shape[0] // width, held.shape[1])
    keep, *sends = pl.pallas_call(
        functools.partial(halve_kernel, index, inner),
        out_shape=[jax.ShapeDtypeStruct(shape, kind) for kind in [F32] + [BF16] * (width - 1)],
        in_specs=[VMEM] * 3,
        out_specs=[VMEM] * width,
        compiler_params=pltpu.CompilerParams(vmem_limit_bytes=2 << 20),
        cost_estimate=pl.CostEstimate(flops=held.size, bytes_accessed=6 * held.size, transcendentals=0),
        name="halve",
    )(flags, held, got)
    return keep, sends


def scatter_sum(keep, send, flags, peers, cols):
    got = swap(send, peers, 1)
    keep, sends = halved(flags, keep, got, 1, LINE * cols)
    got = swap(sends[0], peers, 2 + SIDE_FLIP)
    keep, sends = halved(flags, keep, got, LOW.bit_length() - 1, cols, LINE)
    for got in exchanged(sends, peers):
        keep = keep + got.astype(F32)
    return keep


def plain_latent(latent, weight_mix, weight_out):
    whole = lax.all_gather(latent, "rows", axis=0, tiled=True)

    def conv(value, weight):
        rows, cols = value.shape[:2]
        padded = jnp.pad(value, ((1, 1), (1, 1), (0, 0)))
        summed = 0.0
        for a in range(3):
            for b in range(3):
                summed = summed + jnp.dot(
                    padded[a : a + rows, b : b + cols], weight[a, b], preferred_element_type=F32
                )
        return summed

    hidden = jax.nn.silu(conv(whole, weight_mix)).astype(BF16)
    mixed = lax.psum_scatter(conv(hidden, weight_out), "rows", scatter_dimension=0, tiled=True)
    return (latent.astype(F32) + mixed).astype(BF16)


def compute(pixels, weight_first, weight_second, weight_mix, weight_out):
    peers = lax.axis_size("rows")
    me = lax.axis_index("rows")
    flags, spread = placed(me, peers)
    inner, outer = halo(pixels, peers, lax.axis_size("groups"))
    latent = image_stage(flags, spread, inner, outer, pixels, weight_first, weight_second)
    if peers != LINE * LOW or latent.shape[0] != 1 or weight_mix.shape[3] % LANES:
        return plain_latent(latent, weight_mix, weight_out)
    cols = latent.shape[1]
    gathered = gather_rows(latent[0], flags, peers, cols)
    keep, send = latent_stage(flags, gathered, weight_mix, weight_out, cols)
    mixed = scatter_sum(keep, send, flags, peers, cols)
    return (latent.astype(F32) + mixed[None]).astype(BF16)


def solution(mesh):
    return jax.shard_map(
        compute,
        mesh=mesh,
        in_specs=(
            P(("groups", "rows"), None, None),
            P(),
            P(),
            P(None, None, None, "rows"),
            P(None, None, "rows", None),
        ),
        out_specs=P(("groups", "rows"), None, None),
        check_vma=False,
    )
```

```python
import functools

import jax
import jax.numpy as jnp
from jax import lax
from jax.experimental import pallas as pl
from jax.experimental.pallas import tpu as pltpu
from jax.sharding import PartitionSpec as P


F32 = jnp.float32
BF16 = jnp.bfloat16
LOW = 4
LOW_ORDER = (0, 2, 1, 3)
LINE = 4
NEAR_FLIP, FAR_FLIP, SIDE_FLIP = 0, 1, 1
LANES = 128
VMEM = pl.BlockSpec(memory_space=pltpu.VMEM)
COVER = 2 * 10**10


def silu(value):
    return value / (1.0 + jnp.exp(-value))


def flag_of(flags_ref, index):
    return flags_ref[index, :1, :1] != 0


def pick(flag, one, other):
    return jnp.where(flag, one.astype(F32), other.astype(F32))


def kind_of(core, side, place):
    return core ^ (SIDE_FLIP * side) ^ (NEAR_FLIP * (place & 1)) ^ (FAR_FLIP * (place >> 1))


def place_kernel(bits, last, me_ref, flags_ref, spread_ref):
    me = me_ref[...]
    for bit in range(bits):
        flags_ref[bit] = (me >> bit) & 1
    flags_ref[bits] = (me == 0).astype(jnp.int32)
    flags_ref[bits + 1] = (me == last).astype(jnp.int32)
    flags_ref[bits + 2] = kind_of(me & 1, (me >> 1) & 1, (me >> 2) & 3)
    shape = (LANES, spread_ref.shape[1])
    source = lax.broadcasted_iota(jnp.int32, shape, 0)
    target = lax.broadcasted_iota(jnp.int32, shape, 1)
    for r in range(4):
        place = target == 4 * source + 2 * (r % 2) + r // 2
        spread_ref[r * LANES : (r + 1) * LANES] = place.astype(F32).astype(spread_ref.dtype)


def placed(me, peers):
    bits = max(1, (peers - 1).bit_length())
    return pl.pallas_call(
        functools.partial(place_kernel, bits, peers - 1),
        out_shape=[
            jax.ShapeDtypeStruct((bits + 3, 8, LANES), jnp.int32),
            jax.ShapeDtypeStruct((4 * LANES, 4 * LANES), BF16),
        ],
        in_specs=[VMEM],
        out_specs=[VMEM] * 2,
        compiler_params=pltpu.CompilerParams(vmem_limit_bytes=2 << 20),
        cost_estimate=pl.CostEstimate(flops=COVER, bytes_accessed=0, transcendentals=0),
        name="place",
    )(jnp.broadcast_to(me, (8, LANES)))


def shift_cols(value, step, width):
    if step == 0:
        return value
    count = value.shape[0]
    moved = pltpu.roll(value, (-step) % count, 0)
    col = lax.broadcasted_iota(jnp.int32, value.shape, 0) % width
    keep = (col + step >= 0) & (col + step < width)
    return jnp.where(keep, moved, 0.0)


def conv_image(feature, weight_ref, width):
    out_rows = feature.shape[0] - 2 * width
    total = None
    for col_tap in (0, 2, 1):
        term = None
        for row_tap in range(3):
            part = jnp.dot(
                feature[row_tap * width : row_tap * width + out_rows],
                weight_ref[row_tap, col_tap],
                preferred_element_type=F32,
            )
            term = part if term is None else term + part
        term = shift_cols(term, col_tap - 1, width)
        total = term if total is None else total + term
    return total


def averaged(value_ref, chunk, count):
    first, second = value_ref[chunk, pl.ds(0, count, stride=2), :], value_ref[chunk, pl.ds(1, count, stride=2), :]
    return ((first + second) * 0.5).astype(BF16).astype(F32)


def first_kernel(flags_ref, inner_ref, outer_ref, pixels_ref, first_ref, activated_ref):
    rows, width, chans = pixels_ref.shape
    flat = lambda ref: ref[...].reshape(ref.shape[0] * width, chans)
    pixels = flat(pixels_ref)
    odd, bits = flag_of(flags_ref, 0), flags_ref.shape[0] - 3
    inner, outer = flat(inner_ref), flat(outer_ref)
    edge = 2 * width
    before = pick(odd, inner[-edge:], outer[-edge:]).astype(BF16)
    after = pick(odd, outer[:edge], inner[:edge]).astype(BF16)
    before = jnp.where(flag_of(flags_ref, bits), 0.0, before.astype(F32)).astype(BF16)
    after = jnp.where(flag_of(flags_ref, bits + 1), 0.0, after.astype(F32)).astype(BF16)
    extended = jnp.concatenate([before, pixels, after], axis=0)
    activated = silu(conv_image(extended, first_ref, width)).astype(BF16).astype(F32)
    row = lax.broadcasted_iota(jnp.int32, activated.shape, 0) // width
    inside = (row >= flags_ref[bits, :1, :1]) & (row < rows + 2 - flags_ref[bits + 1, :1, :1])
    activated_ref[...] = jnp.where(inside, activated, 0.0).astype(BF16)


def second_kernel(activated_ref, pixels_ref, spread_ref, second_ref, latent_ref, wide_ref, half_ref, packed_ref):
    rows, width, chans = pixels_ref.shape
    pixels = pixels_ref[...].reshape(rows * width, chans)
    block = pixels.astype(F32) + conv_image(activated_ref[...], second_ref, width)
    block = block.astype(BF16).astype(F32)
    count = rows * width
    chunks = chans // LANES
    cols = width // 4
    for chunk in range(chunks):
        wide_ref[chunk] = block[:, chunk * LANES : (chunk + 1) * LANES]
    for chunk in range(chunks):
        half_ref[chunk] = averaged(wide_ref, chunk, count // 2)
    quarters = [averaged(half_ref, chunk, count // 4) for chunk in range(chunks)]
    for out_row in range(rows // 4):
        for chunk in range(chunks):
            for sub in range(4):
                start = (4 * out_row + sub) * cols
                packed_ref[chunk * cols : (chunk + 1) * cols, sub * LANES : (sub + 1) * LANES] = quarters[chunk][
                    start : start + cols
                ]
        latent = jnp.dot(packed_ref[...].astype(BF16), spread_ref[...], preferred_element_type=F32)
        for chunk in range(chunks):
            latent_ref[out_row, :, chunk * 4 * LANES : (chunk + 1) * 4 * LANES] = latent[
                chunk * cols : (chunk + 1) * cols
            ].astype(BF16)


def image_stage(flags, spread, inner, outer, pixels, weight_first, weight_second):
    rows, width, chans = pixels.shape
    cost = lambda count, weight: pl.CostEstimate(
        flops=2 * count * weight.size, bytes_accessed=2 * weight.size + 6 * pixels.size, transcendentals=0
    )
    activated = pl.pallas_call(
        first_kernel,
        out_shape=jax.ShapeDtypeStruct(((rows + 2) * width, chans), BF16),
        in_specs=[VMEM] * 5,
        out_specs=VMEM,
        compiler_params=pltpu.CompilerParams(vmem_limit_bytes=16 << 20),
        cost_estimate=cost((rows + 2) * width, weight_first),
        name="first_stage",
    )(flags, inner, outer, pixels, weight_first)
    return pl.pallas_call(
        second_kernel,
        out_shape=jax.ShapeDtypeStruct((rows // 4, width // 4, 4 * chans), BF16),
        in_specs=[VMEM] * 4,
        out_specs=VMEM,
        scratch_shapes=[
            pltpu.VMEM((chans // LANES, rows * width, LANES), F32),
            pltpu.VMEM((chans // LANES, rows * width // 2, LANES), F32),
            pltpu.VMEM((chans // LANES * (width // 4), 4 * LANES), F32),
        ],
        compiler_params=pltpu.CompilerParams(vmem_limit_bytes=16 << 20),
        cost_estimate=cost(rows * width, weight_second),
        name="image_stage",
    )(activated, pixels, spread, weight_second)


def shift_rows(value, step, block, cols):
    if step == 0:
        return value
    pieces = [value[LOW_ORDER[u] * block : (LOW_ORDER[u] + 1) * block] for u in range(LOW)]
    high = lax.broadcasted_iota(jnp.int32, pieces[0].shape, 0) // cols
    if step > 0:
        wrapped = jnp.where(high < block // cols - 1, pltpu.roll(pieces[0], block - cols, 0), 0.0)
        pieces = pieces[1:] + [wrapped]
    else:
        wrapped = jnp.where(high > 0, pltpu.roll(pieces[-1], cols, 0), 0.0)
        pieces = [wrapped] + pieces[:-1]
    return jnp.concatenate([pieces[u] for u in LOW_ORDER], axis=0)


SPOTS = [(side, place) for side in range(LOW // 2) for place in range(LINE)]


def block_of(value, core, side, place, cols):
    start = ((core * (LOW // 2) + side) * LINE + place) * cols
    return value[start : start + cols]


def halve(total, flags, inner, keep_ref, *send_refs):
    width = len(send_refs) + 1
    for run in range(total.shape[0] // (width * inner)):
        parts = [total[(width * run + k) * inner : (width * run + k + 1) * inner] for k in range(width)]
        for bit, flag in enumerate(flags):
            parts = [jnp.where(flag, parts[k ^ (1 << bit)], parts[k]) for k in range(width)]
        keep_ref[run * inner : (run + 1) * inner] = parts[0]
        for part, send_ref in zip(parts[1:], send_refs):
            send_ref[run * inner : (run + 1) * inner] = part.astype(send_ref.dtype)


def latent_kernel(cols, flags_ref, own_ref, got_ref, mix_ref, out_ref, keep_ref, send_ref, gathered_ref):
    unite_kernel(flags_ref, own_ref, got_ref, gathered_ref)
    feature = gathered_ref[...]
    block = feature.shape[0] // LOW
    hidden_count = mix_ref.shape[3]
    taps = [(a, b) for a in range(3) for b in range(3)]
    terms = {}
    for start in range(0, 9, 2):
        pair = taps[start : start + 2]
        weight = jnp.concatenate([mix_ref[a, b] for a, b in pair], axis=1)
        both = jnp.dot(feature, weight, preferred_element_type=F32)
        for slot, tap in enumerate(pair):
            terms[tap] = both[:, slot * hidden_count : (slot + 1) * hidden_count]
    summed = None
    for a in range(3):
        line = terms[a, 1] + shift_cols(terms[a, 0], -1, cols) + shift_cols(terms[a, 2], 1, cols)
        line = shift_rows(line, a - 1, block, cols)
        summed = line if summed is None else summed + line
    hidden = silu(summed).astype(BF16).astype(F32)
    moved = []
    for a in range(3):
        line = shift_rows(hidden, a - 1, block, cols)
        for b in range(3):
            moved.append(shift_cols(line, b - 1, cols).astype(BF16))
    stacked = jnp.concatenate(moved, axis=1)
    weight = out_ref[...].reshape(9 * hidden_count, out_ref.shape[3])
    total = jnp.dot(stacked, weight, preferred_element_type=F32)
    kind = flag_of(flags_ref, flags_ref.shape[0] - 1)
    for index, (side, place) in enumerate(SPOTS):
        first, second = [block_of(total, kind_of(which, side, place), side, place, cols) for which in range(2)]
        keep_ref[index * cols : (index + 1) * cols] = pick(kind, second, first)
        send_ref[index * cols : (index + 1) * cols] = pick(kind, first, second).astype(send_ref.dtype)


def latent_stage(flags, own, got, weight_mix, weight_out, cols):
    count, chans = 2 * own.shape[0], own.shape[1]
    flops = 2 * count * (weight_mix.size + weight_out.size)
    moved = 2 * (weight_mix.size + weight_out.size) + 6 * count * chans
    return pl.pallas_call(
        functools.partial(latent_kernel, cols),
        out_shape=[jax.ShapeDtypeStruct((count // 2, chans), kind) for kind in (F32, BF16)],
        in_specs=[VMEM] * 5,
        out_specs=[VMEM] * 2,
        scratch_shapes=[pltpu.VMEM((count, chans), BF16)],
        compiler_params=pltpu.CompilerParams(vmem_limit_bytes=20 << 20),
        cost_estimate=pl.CostEstimate(flops=flops, bytes_accessed=moved, transcendentals=count * weight_mix.shape[3]),
        name="latent_stage",
    )(flags, own, got, weight_mix, weight_out)


def swap(value, peers, bit):
    return lax.ppermute(value, "rows", [(i, i ^ bit) for i in range(peers)])


def halo(value, peers, groups):
    got = []
    for first in (0, 1):
        partner = {}
        for i in range(first, peers - 1, 2):
            partner[i], partner[i + 1] = i + 1, i
        pairs = []
        for group in range(groups):
            for i in range(peers):
                if i in partner:
                    pairs.append((group * peers + i, group * peers + partner[i]))
                elif group ^ 1 < groups:
                    pairs.append((group * peers + i, (group ^ 1) * peers + i))
        got.append(lax.ppermute(value, ("groups", "rows"), pairs))
    return got


def merge_kernel(index, inner, flags_ref, *refs):
    *blocks, both_ref = refs
    width = len(blocks)
    flags = [flag_of(flags_ref, index + bit) for bit in range((width - 1).bit_length())]
    values = [ref[...].astype(F32) for ref in blocks]
    for block in range(values[0].shape[0] // inner):
        parts = [value[block * inner : (block + 1) * inner] for value in values]
        for bit, flag in enumerate(flags):
            parts = [jnp.where(flag, parts[k ^ (1 << bit)], parts[k]) for k in range(width)]
        for k, part in enumerate(parts):
            start = (width * block + k) * inner
            both_ref[start : start + inner] = part.astype(both_ref.dtype)


def unite_kernel(flags_ref, own_ref, got_ref, both_ref):
    kind = flag_of(flags_ref, flags_ref.shape[0] - 1)
    own, got = own_ref[...].astype(F32), got_ref[...].astype(F32)
    kinds = [pick(kind, got, own), pick(kind, own, got)]
    cols = own.shape[0] // len(SPOTS)
    for index, (side, place) in enumerate(SPOTS):
        for core in range(2):
            start = ((core * (LOW // 2) + side) * LINE + place) * cols
            block = kinds[kind_of(core, side, place)][index * cols : (index + 1) * cols]
            both_ref[start : start + cols] = block.astype(both_ref.dtype)


def merged(flags, blocks, index, inner, cover=0):
    rows, chans = blocks[0].shape
    return pl.pallas_call(
        functools.partial(merge_kernel, index, inner),
        out_shape=jax.ShapeDtypeStruct((len(blocks) * rows, chans), blocks[0].dtype),
        in_specs=[VMEM] * (1 + len(blocks)),
        out_specs=VMEM,
        compiler_params=pltpu.CompilerParams(vmem_limit_bytes=2 << 20),
        cost_estimate=pl.CostEstimate(flops=cover, bytes_accessed=8 * blocks[0].size, transcendentals=0),
        name="merge",
    )(flags, *blocks)


def exchanged(values, peers):
    got = []
    for k, value in enumerate(values, 1):
        got.append(swap(value, peers, LOW * k + kind_of(0, 0, k)))
    return got


def gather_rows(latent, flags, peers, cols):
    held = merged(flags, [latent, *exchanged([latent] * (LINE - 1), peers)], LOW.bit_length() - 1, cols, COVER)
    held = merged(flags, [held, swap(held, peers, 2 + SIDE_FLIP)], 1, held.shape[0])
    return held, swap(held, peers, 1)


def halve_kernel(index, inner, flags_ref, held_ref, got_ref, keep_ref, *send_refs):
    flags = [flag_of(flags_ref, index + bit) for bit in range(len(send_refs).bit_length())]
    halve(held_ref[...] + got_ref[...].astype(F32), flags, inner, keep_ref, *send_refs)


def halved(flags, held, got, index, inner, width=2):
    shape = (held.shape[0] // width, held.shape[1])
    keep, *sends = pl.pallas_call(
        functools.partial(halve_kernel, index, inner),
        out_shape=[jax.ShapeDtypeStruct(shape, kind) for kind in [F32] + [BF16] * (width - 1)],
        in_specs=[VMEM] * 3,
        out_specs=[VMEM] * width,
        compiler_params=pltpu.CompilerParams(vmem_limit_bytes=2 << 20),
        cost_estimate=pl.CostEstimate(flops=held.size, bytes_accessed=6 * held.size, transcendentals=0),
        name="halve",
    )(flags, held, got)
    return keep, sends


def scatter_sum(keep, send, flags, peers, cols):
    got = swap(send, peers, 1)
    keep, sends = halved(flags, keep, got, 1, LINE * cols)
    got = swap(sends[0], peers, 2 + SIDE_FLIP)
    keep, sends = halved(flags, keep, got, LOW.bit_length() - 1, cols, LINE)
    for got in exchanged(sends, peers):
        keep = keep + got.astype(F32)
    return keep


def plain_latent(latent, weight_mix, weight_out):
    whole = lax.all_gather(latent, "rows", axis=0, tiled=True)

    def conv(value, weight):
        rows, cols = value.shape[:2]
        padded = jnp.pad(value, ((1, 1), (1, 1), (0, 0)))
        summed = 0.0
        for a in range(3):
            for b in range(3):
                summed = summed + jnp.dot(
                    padded[a : a + rows, b : b + cols], weight[a, b], preferred_element_type=F32
                )
        return summed

    hidden = jax.nn.silu(conv(whole, weight_mix)).astype(BF16)
    mixed = lax.psum_scatter(conv(hidden, weight_out), "rows", scatter_dimension=0, tiled=True)
    return (latent.astype(F32) + mixed).astype(BF16)


def compute(pixels, weight_first, weight_second, weight_mix, weight_out):
    peers = lax.axis_size("rows")
    me = lax.axis_index("rows")
    flags, spread = placed(me, peers)
    inner, outer = halo(pixels, peers, lax.axis_size("groups"))
    latent = image_stage(flags, spread, inner, outer, pixels, weight_first, weight_second)
    if peers != LINE * LOW or latent.shape[0] != 1 or weight_mix.shape[3] % LANES:
        return plain_latent(latent, weight_mix, weight_out)
    cols = latent.shape[1]
    own, got = gather_rows(latent[0], flags, peers, cols)
    keep, send = latent_stage(flags, own, got, weight_mix, weight_out, cols)
    mixed = scatter_sum(keep, send, flags, peers, cols)
    return (latent.astype(F32) + mixed[None]).astype(BF16)


def solution(mesh):
    return jax.shard_map(
        compute,
        mesh=mesh,
        in_specs=(
            P(("groups", "rows"), None, None),
            P(),
            P(),
            P(None, None, None, "rows"),
            P(None, None, "rows", None),
        ),
        out_specs=P(("groups", "rows"), None, None),
        check_vma=False,
    )
```
